256 devices in a mesh: chain: 128 (over x, z, y), side: 2 (over core).
Axes of the slice: x: 4, y: 4, z: 8, core: 2. Of those that a mesh axis runs over, the one named last changes fastest.
Arguments:
- rhs: float32 [8, 262144], P(None, ('chain', 'side')), may hold values from -0.3 to 0.3
- lower_blocks: bfloat16 [4096, 13, 4096], P(('chain', 'side')), may hold values from -0.03 to 0.03
- lower_cols: int32 [4096, 13], P(('chain', 'side')), may hold values from -1 to 14, as said below
- upper_blocks: bfloat16 [4096, 13, 4096], P(('chain', 'side')), may hold values from -0.03 to 0.03
- upper_cols: int32 [4096, 13], P(('chain', 'side')), may hold values from -1 to 15, as said below
- diag_inverse: bfloat16 [4096, 4096], P(('chain', 'side')), may hold values from -0.375 to 1.25, as said below
- link_lower: bfloat16 [4096, 4096], P(('chain', 'side')), may hold values from -1 to 1
- link_upper: bfloat16 [4096, 4096], P(('chain', 'side')), may hold values from -4 to 4
- row_counts: int32 [256], P(('chain', 'side')), may hold values from 8 to 16, as said below
Outputs:
- solution: float32 [8, 262144], P(None, ('chain', 'side'))
The draws below stay inside these ranges and needn't reach their ends.
Inputs may be any that keep to these rules, and one draw needn't show every extreme that they name: `lower_cols`: entry e of block row k (k counted within its slab) is -1 or a row of the same slab before k; entry 0 is k - 1, or -1 when k is 0. `upper_cols`: entry e of block row k (k counted within its slab) is -1 or a row of the same slab after k; entry 0 is k + 1, or -1 when k is 15. The first row_counts[d] block rows of slab d are active. `diag_inverse`: block g is the inverse of block row g's pivot.
All inputs are finite; a program needn't handle non-finite values.
Results may differ from the reference program's by a relative error of at most 0.00085.
Values sent between devices are 32-bit elements; how exact they have to be, the bound alone decides.
A program may use at most 64 MiB of HBM per device.

```python
import math
import jax
import jax.numpy as jnp
from jax import lax

NODE_UNKNOWNS = 64
R = 8
KL = 13
NB = 16
DEVS = 256
NBT = 4096
COLS = 262144


mixing_share = 0.06


relay_gain = 0.01


def noise_field(key, shape):
    values = jnp.clip(jax.random.normal(key, shape, jnp.float32), -3.0, 3.0)
    return values


def link_transfer_rates(key, start_shift):
    key_order = jax.random.fold_in(key, start_shift + 1)
    key_slow = jax.random.fold_in(key, start_shift + 2)
    key_fast = jax.random.fold_in(key, start_shift + 3)
    key_spread = jax.random.fold_in(key, start_shift + 4)
    key_place = jax.random.fold_in(key, start_shift + 5)
    key_surge = jax.random.fold_in(key, start_shift + 6)
    slow_count = NODE_UNKNOWNS // 2
    order = jax.random.permutation(key_order, NODE_UNKNOWNS)
    place = jnp.zeros((NODE_UNKNOWNS,), jnp.int32).at[order].set(jnp.arange(NODE_UNKNOWNS, dtype=jnp.int32))
    slow = place < slow_count
    slow_total = jnp.exp(jax.random.uniform(key_slow, (NODE_UNKNOWNS,), jnp.float32, math.log(0.1), math.log(0.4)))
    fast_step = jnp.exp(jax.random.uniform(key_fast, (NODE_UNKNOWNS,), jnp.float32, math.log(0.2), math.log(0.7)))
    base = jnp.where(slow, slow_total / DEVS, fast_step)
    spread = jnp.exp(jax.random.uniform(key_spread, (DEVS, NODE_UNKNOWNS), jnp.float32, math.log(0.5), math.log(2.0)))
    places = jax.random.permutation(key_place, DEVS)[:2]
    transfer_losses = jax.random.uniform(key_surge, (2, NODE_UNKNOWNS), jnp.float32, 0.6, 0.8)
    factor = jnp.ones((DEVS, NODE_UNKNOWNS), jnp.float32).at[places].set(transfer_losses)
    rates = jnp.exp(-base[None, :] * spread) * factor
    return (jnp.repeat(rates, NB, axis=0), slow)


def mixing_blocks(key, slow):
    noise = noise_field(key, (NBT, NODE_UNKNOWNS, NODE_UNKNOWNS))
    skew = (noise - jnp.swapaxes(noise, 1, 2)) / math.sqrt(2.0 * NODE_UNKNOWNS)
    identity = jnp.eye(NODE_UNKNOWNS, dtype=jnp.float32)
    blocks = math.sqrt(1.0 - mixing_share) * identity[None] + math.sqrt(mixing_share) * skew
    weights = jnp.where(slow, 1.0, 0.0).astype(jnp.float32)
    squared = blocks * blocks
    kept_slow = jnp.sum(squared * weights[None, :, None], axis=1)
    kept_all = jnp.sum(squared, axis=1)
    share = jnp.mean(weights)
    kept = jnp.where(slow[None, :], kept_slow + relay_gain * share, kept_all + relay_gain)
    return (blocks, kept)


def pivot_inverse(key):
    key_pivot = jax.random.fold_in(key, 41)
    key_spread = jax.random.fold_in(key, 42)
    pivots = jnp.exp(jax.random.uniform(key_pivot, (NBT, NODE_UNKNOWNS), jnp.float32, math.log(0.625), math.log(1.25)))
    spread = jax.random.normal(key_spread, (NBT, NODE_UNKNOWNS, NODE_UNKNOWNS), jnp.float32) * (0.25 / NODE_UNKNOWNS ** 0.5)
    spread = jnp.clip(spread, -0.375, 0.375)
    identity = jnp.eye(NODE_UNKNOWNS, dtype=jnp.float32)
    return spread * (1.0 - identity) + identity * pivots[:, :, None]


def draw_diag_inverse(key, part):
    return pivot_inverse(key).reshape(NBT, NODE_UNKNOWNS * NODE_UNKNOWNS).astype(jnp.bfloat16)


def draw_link_lower(key, part):
    rates, slow = link_transfer_rates(key, 100)
    blocks, kept = mixing_blocks(jax.random.fold_in(key, 110), slow)
    scaled = blocks * (rates / jnp.sqrt(kept))[:, None, :]
    return jnp.clip(scaled, -1.0, 1.0).reshape(NBT, NODE_UNKNOWNS * NODE_UNKNOWNS).astype(jnp.bfloat16)


def draw_link_upper(key, part):
    rates, slow = link_transfer_rates(key, 200)
    blocks, kept = mixing_blocks(jax.random.fold_in(key, 210), slow)
    target = -blocks * (rates / jnp.sqrt(kept))[:, None, :]
    stored = lax.optimization_barrier(pivot_inverse(key).astype(jnp.bfloat16))
    inverse = stored.astype(jnp.float32)
    coupling = jnp.linalg.solve(inverse, target)
    return jnp.clip(coupling, -4.0, 4.0).reshape(NBT, NODE_UNKNOWNS * NODE_UNKNOWNS).astype(jnp.bfloat16)


def draw_lower_blocks(key, part):
    noise = noise_field(jax.random.fold_in(key, 51), (NBT, KL, NODE_UNKNOWNS * NODE_UNKNOWNS))
    return (noise * (1000.0 * NODE_UNKNOWNS) ** (-0.5)).astype(jnp.bfloat16)


def draw_upper_blocks(key, part):
    noise = noise_field(jax.random.fold_in(key, 52), (NBT, KL, NODE_UNKNOWNS * NODE_UNKNOWNS))
    return (noise * (1000.0 * NODE_UNKNOWNS) ** (-0.5)).astype(jnp.bfloat16)


def draw_lower_cols(key, part):
    position = (jnp.arange(NBT, dtype=jnp.int32) % NB)[:, None]
    key_pick = jax.random.fold_in(key, 11)
    key_skip = jax.random.fold_in(key, 12)
    chosen = jax.random.randint(key_pick, (NBT, KL), 0, 1 << 20, dtype=jnp.int32) % jnp.maximum(position, 1)
    skipped = jax.random.randint(key_skip, (NBT, KL), 0, 4, dtype=jnp.int32) == 0
    columns = jnp.where(skipped | (position == 0), -1, chosen)
    columns = columns.at[:, 0].set(jnp.where(position[:, 0] > 0, position[:, 0] - 1, -1))
    return columns.astype(jnp.int32)


def draw_upper_cols(key, part):
    position = (jnp.arange(NBT, dtype=jnp.int32) % NB)[:, None]
    remaining = NB - 1 - position
    key_pick = jax.random.fold_in(key, 21)
    key_skip = jax.random.fold_in(key, 22)
    chosen = position + 1 + jax.random.randint(key_pick, (NBT, KL), 0, 1 << 20, dtype=jnp.int32) % jnp.maximum(remaining, 1)
    skipped = jax.random.randint(key_skip, (NBT, KL), 0, 4, dtype=jnp.int32) == 0
    columns = jnp.where(skipped | (remaining == 0), -1, chosen)
    columns = columns.at[:, 0].set(jnp.where(remaining[:, 0] > 0, position[:, 0] + 1, -1))
    return columns.astype(jnp.int32)


def draw_row_counts(key, part):
    key_count = jax.random.fold_in(key, 31)
    key_order = jax.random.fold_in(key, 32)
    counts = jax.random.randint(key_count, (DEVS,), NB // 2, NB + 1, dtype=jnp.int32)
    order = jax.random.permutation(key_order, DEVS)
    counts = counts.at[order[0]].set(NB).at[order[1]].set(NB // 2)
    return counts.astype(jnp.int32)


def levels(stream_key, extent, shards, least, top_value):
    factor_of, own = 1.0, jax.random.fold_in(stream_key, 6)
    for dim, shards_of in shards:
        draws = jnp.exp(jax.random.uniform(jax.random.fold_in(own, dim), (shards_of,), jnp.float32, least / len(shards), top_value / len(shards)))
        factor_of = factor_of * jnp.repeat(draws, extent[dim] // shards_of).reshape([-1 if axis == dim else 1 for axis in range(len(extent))])
    return factor_of


def bell_draw(rng, extent, width, bound, split=(), kind=jnp.bfloat16):
    entries = jax.random.normal(rng, extent, jnp.float32) * width
    if len(split) > 0:
        entries = levels(rng, extent, split, -0.22, 0.18) * entries
    return jnp.clip(entries, min=-bound, max=bound).astype(kind)


def setup_inputs(seed: int = 0) -> dict:
    arg_keys = jax.random.split(jax.random.key(seed), 10)
    rhs = bell_draw(arg_keys[0], (R, COLS), 0.05, 0.3, ((1, 256),), jnp.float32)
    lower_blocks = draw_lower_blocks(jax.random.fold_in(arg_keys[9], 71), 0)
    lower_cols = draw_lower_cols(jax.random.fold_in(arg_keys[9], 71), 0)
    upper_blocks = draw_upper_blocks(jax.random.fold_in(arg_keys[9], 71), 0)
    upper_cols = draw_upper_cols(jax.random.fold_in(arg_keys[9], 71), 0)
    diag_inverse = draw_diag_inverse(jax.random.fold_in(arg_keys[9], 71), 0)
    link_lower = draw_link_lower(jax.random.fold_in(arg_keys[9], 71), 0)
    link_upper = draw_link_upper(jax.random.fold_in(arg_keys[9], 71), 0)
    row_counts = draw_row_counts(jax.random.fold_in(arg_keys[9], 71), 0)
    return {"rhs": rhs, "lower_blocks": lower_blocks, "lower_cols": lower_cols, "upper_blocks": upper_blocks, "upper_cols": upper_cols, "diag_inverse": diag_inverse, "link_lower": link_lower, "link_upper": link_upper, "row_counts": row_counts}


def product(vector, matrix):
    return jnp.dot(vector, matrix.T, precision=lax.Precision.HIGHEST)

def reference(rhs, lower_blocks, lower_cols, upper_blocks, upper_cols, diag_inverse, link_lower, link_upper, row_counts):
    slab_rhs = rhs.reshape(R, DEVS, NB, NODE_UNKNOWNS).transpose(1, 2, 0, 3)
    lower = lower_blocks.astype(jnp.float32).reshape(DEVS, NB, KL, NODE_UNKNOWNS, NODE_UNKNOWNS)
    upper = upper_blocks.astype(jnp.float32).reshape(DEVS, NB, KL, NODE_UNKNOWNS, NODE_UNKNOWNS)
    inverses = diag_inverse.astype(jnp.float32).reshape(DEVS, NB, NODE_UNKNOWNS, NODE_UNKNOWNS)
    links_down = link_lower.astype(jnp.float32).reshape(DEVS, NB, NODE_UNKNOWNS, NODE_UNKNOWNS)
    links_up = link_upper.astype(jnp.float32).reshape(DEVS, NB, NODE_UNKNOWNS, NODE_UNKNOWNS)
    lower_lists = lower_cols.reshape(DEVS, NB, KL)
    upper_lists = upper_cols.reshape(DEVS, NB, KL)

    def forward_slab(carried_partial, slab):
        values, blocks, columns, link, active_rows = slab

        def one_row(row_index, solved):
            total = values[row_index] - product(carried_partial, link[row_index])
            for entry in range(KL):
                column = columns[row_index, entry]
                other = solved[jnp.maximum(column, 0)]
                total = jnp.where(column >= 0, total - product(other, blocks[row_index, entry]), total)
            return solved.at[row_index].set(jnp.where(row_index < active_rows, total, jnp.zeros_like(total)))
        solved = lax.fori_loop(0, NB, one_row, jnp.zeros((NB, R, NODE_UNKNOWNS), jnp.float32))
        return (solved[active_rows - 1], solved)
    last_forward, forward_direction = lax.scan(forward_slab, jnp.zeros((R, NODE_UNKNOWNS), jnp.float32), (slab_rhs, lower, lower_lists, links_down, row_counts))

    def backward_slab(carried_partial, slab):
        values, blocks, columns, link, inverse, active_rows = slab

        def one_row(step, solved):
            row_index = NB - 1 - step
            total = values[row_index] - product(carried_partial, link[row_index])
            for entry in range(KL):
                column = columns[row_index, entry]
                other = solved[jnp.maximum(column, 0)]
                total = jnp.where(column >= 0, total - product(other, blocks[row_index, entry]), total)
            total = product(total, inverse[row_index])
            return solved.at[row_index].set(jnp.where(row_index < active_rows, total, jnp.zeros_like(total)))
        solved = lax.fori_loop(0, NB, one_row, jnp.zeros((NB, R, NODE_UNKNOWNS), jnp.float32))
        return (solved[0], solved)
    first_backward, backward = lax.scan(backward_slab, jnp.zeros((R, NODE_UNKNOWNS), jnp.float32), (forward_direction, upper, upper_lists, links_up, inverses, row_counts), reverse=True)
    return backward.transpose(2, 0, 1, 3).reshape(R, COLS)
```

```python
import functools

import jax
import jax.numpy as jnp
from jax import lax
from jax.experimental import pallas as pl
from jax.experimental.pallas import tpu as pltpu
from jax.sharding import PartitionSpec as P

U = 64
R = 8
NB = 16
KL = 13
F32 = jnp.float32
BF16 = jnp.bfloat16
MESH = pl.DeviceIdType.MESH
NT = (((1,), (1,)), ((), ()))
NN = (((1,), (0,)), ((), ()))
LEVELS = (4, 8, 4)


def split(x):
    hi = x.astype(BF16)
    return hi, (x - hi.astype(F32)).astype(BF16)


def mm(a, b, dims):
    return lax.dot_general(a, b, dims, preferred_element_type=F32)


def dot3(x, w, dims=NN):
    m = x.shape[0]
    xh, xl = split(x)
    wh, wl = split(w)
    both = mm(jnp.concatenate([xh, xl], axis=0), wh, dims)
    return both[:m] + both[m:] + mm(xh, wl, dims)


def dot2(x, w, dims=NN):
    m = x.shape[0]
    xh, xl = split(x)
    both = mm(jnp.concatenate([xh, xl], axis=0), w, dims)
    return both[:m] + both[m:]


def iota(shape, axis):
    return lax.broadcasted_iota(jnp.int32, shape, axis)


def swap_halves(x):
    return pltpu.roll(x, U, axis=1)


def one_hot(cols_ref, active):
    spread = (iota((KL, 256), 1) % 16 == iota((KL, 256), 0)).astype(BF16)
    cols = cols_ref[...].astype(F32).astype(BF16)
    by_row = mm(cols, spread, NN)
    rows = (iota((256, NB), 0) % 16 == iota((256, NB), 1)).astype(BF16)
    listed = mm(rows, by_row.astype(BF16), NN)
    r = iota((256, 256), 0)
    lane = iota((256, 256), 1)
    column = (2 * ((r // 16) % 8) + r // 128).astype(F32)
    keep = (listed == column) & (lane // 16 == r % 16) & (lane % 16 < KL) & (r % 16 < active)
    return jnp.where(keep, 1.0, 0.0).astype(BF16)


def assemble(blocks_ref, cols_ref, active, padded, panel):
    hot = one_hot(cols_ref, active)
    for k in range(NB):
        rows = blocks_ref[k].astype(F32)
        rows = jnp.concatenate([rows, jnp.zeros((16 - KL, U * U), F32)], axis=0)
        padded[pl.ds(16 * k, 16), :] = rows.astype(BF16)
    low = iota((128, 128), 1) < U
    for t in range(16):
        tile = mm(hot, padded[:, pl.ds(256 * t, 256)], NN)
        for s in range(2):
            even = tile[0:128, 128 * s : 128 * s + 128]
            odd = tile[128:256, 128 * s : 128 * s + 128]
            i = 4 * t + 2 * s
            panel[pl.ds(i, 128, stride=U), :] = jnp.where(low, even, swap_halves(odd))
            panel[pl.ds(i + 1, 128, stride=U), :] = jnp.where(low, swap_halves(even), odd)


def spread_rows(flat_ref, out):
    for t in range(32):
        tile = flat_ref[:, pl.ds(128 * t, 128)].astype(F32)
        out[pl.ds(2 * t, NB, stride=U), :] = tile
        out[pl.ds(2 * t + 1, NB, stride=U), :] = swap_halves(tile)


def local_kernel(
    rhs, lower, lcols, upper, ucols, diag, llow, lup, counts, maps, zout,
    padded, pan_l, pan_u, work, dinv, links,
):
    active = counts[0]
    assemble(lower, lcols, active, padded, pan_l)
    assemble(upper, ucols, active, padded, pan_u)
    live = (iota((1, NB * U), 1) // U) < active
    eye = (iota((U, U), 0) == iota((U, U), 1)).astype(BF16)
    spread_rows(llow, links)
    seed = mm(eye, links[:, 0:U].astype(BF16), NT)
    work[0:R, :] = jnp.where(live, rhs[...], 0.0)
    work[R : R + U, :] = jnp.where(live, -seed, 0.0)
    spread_rows(lup, links)
    seed = mm(eye, links[:, 0:U].astype(BF16), NT)
    work[R + U : R + 2 * U, :] = jnp.where(live, -seed, 0.0)
    spread_rows(diag, dinv)
    low = iota((1, 128), 1) < U
    n1 = R + U
    last = jnp.zeros((n1, 128), F32)
    for c in range(8):
        base = c * 1024
        w = work[0:n1, pl.ds(128 * c, 128)]
        x = w - dot3(w, pan_l[pl.ds(base + 128 * c, 128), :], NT)
        work[0:n1, pl.ds(128 * c, 128)] = x
        mine = 2 * c + jnp.where(low, 0, 1) == active - 1
        last = last + jnp.where(mine, x, 0.0)
        rest = 1024 - 128 * (c + 1)
        if rest:
            step = dot3(x, pan_l[pl.ds(base + 128 * (c + 1), rest), :], NT)
            work[0:n1, pl.ds(128 * (c + 1), rest)] -= step
    boundary = last + swap_halves(last)
    z0 = None
    for c in reversed(range(8)):
        base = c * 1024
        v = work[:, pl.ds(128 * c, 128)]
        odd = dot2(v[:, U:128], dinv[pl.ds(128 * c + U, U), 0:U].astype(BF16), NT)
        up = pan_u[pl.ds(base + 128 * c, U), U:128]
        even = v[:, 0:U] - dot3(odd, up, NT)
        even = dot2(even, dinv[pl.ds(128 * c, U), 0:U].astype(BF16), NT)
        z = jnp.concatenate([even, odd], axis=1)
        zout[:, pl.ds(128 * c, 128)] = z
        if c:
            step = dot3(z, pan_u[pl.ds(base, 128 * c), :], NT)
            work[:, pl.ds(0, 128 * c)] -= step
        z0 = z
    maps[0:n1, :] = jnp.where(low, boundary, swap_halves(z0[0:n1]))
    half = n1 + U // 2
    maps[n1:half, :] = jnp.where(low, z0[n1:half], swap_halves(z0[half:]))


def unpack(m):
    low = iota((1, 128), 1) < U
    d = m[R + U :]
    return jnp.concatenate(
        [m[: R + U], jnp.where(low, 0.0, swap_halves(d)), jnp.where(low, 0.0, d)], axis=0
    )


def pack(m):
    low = iota((1, 128), 1) < U
    top, bottom = m[R + U : R + U + U // 2], m[R + U + U // 2 :]
    return jnp.concatenate([m[: R + U], jnp.where(low, swap_halves(top), bottom)], axis=0)


def add_offset(t, m):
    return jnp.concatenate([t[:R] + m[:R], t[R:]], axis=0)


def compose(left, right):
    low = iota((1, 128), 1) < U
    n1 = R + U
    t = add_offset(dot3(left[:n1, :U], right[R:n1]), right)
    weights = jnp.concatenate([jnp.zeros((U, 128), F32), left[n1:]], axis=0)
    s = dot3(jnp.concatenate([t, right[n1:]], axis=0), weights)
    return jnp.concatenate([jnp.where(low, t, s[:n1] + left[:n1]), s[n1:]], axis=0)


def tree(nodes):
    layers = [nodes]
    while len(nodes) > 1:
        nodes = [compose(nodes[i], nodes[i + 1]) for i in range(0, len(nodes), 2)]
        layers.append(nodes)
    return layers


def identity_map():
    r = iota((R + 2 * U, 128), 0)
    lane = iota((R + 2 * U, 128), 1)
    one = ((r >= R) & (r < R + U) & (lane == r - R)) | ((r >= R + U) & (lane == r - R - U + U))
    return jnp.where(one, 1.0, 0.0)


def narrow(layers, index, before, after):
    width = 1
    for nodes in layers[:-1]:
        here = index // width
        sibling = nodes[0]
        for j in range(len(nodes)):
            sibling = jnp.where((here ^ 1) == j, nodes[j], sibling)
        right = here % 2 == 1
        c = compose(jnp.where(right, sibling, after), jnp.where(right, before, sibling))
        before, after = jnp.where(right, c, before), jnp.where(right, after, c)
        width *= 2
    return before, after


def scan_kernel(
    levels, maps, z, out, b_core, b_y, b_z, b_x, s_core, r_core, s_y, r_y, s_z, r_z, s_x, r_x
):
    nx, nz, ny = levels
    chain = lax.axis_index("chain")
    side = lax.axis_index("side")
    y = chain % ny
    zz = (chain // ny) % nz
    x = chain // (ny * nz)

    def at_y(k):
        return (chain - y + (y + k) % ny, side)

    def at_z(k):
        return (chain - zz * ny + ((zz + k) % nz) * ny, side)

    def at_x(k):
        return (((x + k) % nx) * (ny * nz) + chain % (ny * nz), side)

    peers = [(chain, 1 - side)]
    peers += [at_y(k) for k in range(1, ny)]
    peers += [at_z(k) for k in range(1, nz)]
    peers += [at_x(k) for k in range(1, nx)]
    barrier = pltpu.get_barrier_semaphore()
    for peer in peers:
        pl.semaphore_signal(barrier, inc=1, device_id=peer, device_id_type=MESH)
    pl.semaphore_wait(barrier, len(peers))

    def share(value, buf, index, count, peer_of, send, recv):
        buf[index] = value
        order = sorted(range(1, count), key=lambda k: min(k, count - k))
        copies = []
        for k in order:
            copy = pltpu.make_async_remote_copy(
                src_ref=buf.at[index],
                dst_ref=buf.at[index],
                send_sem=send.at[k - 1],
                recv_sem=recv.at[k - 1],
                device_id=peer_of(k),
                device_id_type=MESH,
            )
            copy.start()
            copies.append(copy)
        return copies

    def collect(copies, buf, count):
        for copy in copies:
            copy.wait()
        return [unpack(buf[j]) for j in range(count)]

    copies = share(maps[...], b_core, side, 2, lambda k: (chain, 1 - side), s_core, r_core)
    core_layers = tree(collect(copies, b_core, 2))
    copies = share(pack(core_layers[-1][0]), b_y, y, ny, at_y, s_y, r_y)
    y_layers = tree(collect(copies, b_y, ny))
    copies = share(pack(y_layers[-1][0]), b_z, zz, nz, at_z, s_z, r_z)
    z_layers = tree(collect(copies, b_z, nz))
    copies = share(pack(z_layers[-1][0]), b_x, x, nx, at_x, s_x, r_x)
    before = after = identity_map()
    before, after = narrow(core_layers, side, before, after)
    before, after = narrow(y_layers, y, before, after)
    before, after = narrow(z_layers, zz, before, after)
    groups = collect(copies, b_x, nx)

    n1 = R + U
    t = groups[0][:R]
    p = jnp.zeros((R, U), F32)
    ends = [t]
    for j in range(1, nx):
        p = jnp.where(x == j, t[:, :U], p)
        if j < nx - 1 or True:
            t = dot3(t[:, :U], groups[j][R:n1]) + groups[j][:R]
            ends.append(t)
    q_run = ends[nx - 1][:, U:]
    q = jnp.zeros((R, U), F32)
    for j in reversed(range(nx - 1)):
        q = jnp.where(x == j, q_run, q)
        if j:
            q_run = dot3(q_run, groups[j][n1:, U:]) + ends[j][:, U:]
    own = unpack(maps[...])
    t = dot3(p, before[R:n1, :U]) + before[:R, :U]
    p = t
    t = dot3(p, own[R:n1, :U]) + own[:R, :U]
    t = dot3(t, after[R:n1]) + after[:R]
    q = t[:, U:] + dot3(q, after[n1:, U:])
    pq = jnp.concatenate([p, q], axis=1)
    out[...] = z[0:R, :] + dot3(pq, z[R:, :])


def local(levels, interpret, rhs, lower, lcols, upper, ucols, diag, llow, lup, counts):
    vmem = pl.BlockSpec(memory_space=pltpu.VMEM)
    rows = R + 2 * U
    packed = R + U + U // 2
    maps, z = pl.pallas_call(
        local_kernel,
        out_shape=(
            jax.ShapeDtypeStruct((packed, 128), F32),
            jax.ShapeDtypeStruct((rows, NB * U), F32),
        ),
        in_specs=[vmem] * 8 + [pl.BlockSpec(memory_space=pltpu.SMEM)],
        out_specs=(vmem, vmem),
        scratch_shapes=[
            pltpu.VMEM((256, 4096), BF16),
            pltpu.VMEM((8192, 128), F32),
            pltpu.VMEM((8192, 128), F32),
            pltpu.VMEM((rows, NB * U), F32),
            pltpu.VMEM((NB * U, 128), F32),
            pltpu.VMEM((NB * U, 128), F32),
        ],
        compiler_params=pltpu.CompilerParams(vmem_limit_bytes=48 * 1024 * 1024),
        interpret=interpret,
        name="local_sweeps",
    )(rhs, lower, lcols, upper, ucols, diag, llow, lup, counts)
    if levels is None:
        return maps, z
    nx, nz, ny = levels
    dma = pltpu.SemaphoreType.DMA
    return pl.pallas_call(
        functools.partial(scan_kernel, levels),
        out_shape=jax.ShapeDtypeStruct((R, NB * U), F32),
        in_specs=[vmem, vmem],
        out_specs=vmem,
        scratch_shapes=[pltpu.VMEM((n, packed, 128), F32) for n in (2, ny, nz, nx)]
        + [dma((n - 1,)) for n in (2, 2, ny, ny, nz, nz, nx, nx)],
        compiler_params=pltpu.CompilerParams(
            collective_id=0, has_side_effects=True, vmem_limit_bytes=48 * 1024 * 1024
        ),
        name="slab_scan",
    )(maps, z)


def solution(mesh, levels=LEVELS):
    both = ("chain", "side")
    return jax.shard_map(
        functools.partial(local, levels, False),
        mesh=mesh,
        in_specs=(
            P(None, both),
            P(both, None, None),
            P(both, None),
            P(both, None, None),
            P(both, None),
            P(both, None),
            P(both, None),
            P(both, None),
            P(both),
        ),
        out_specs=P(None, both),
        check_vma=False,
    )
```

```python
import functools

import jax
import jax.numpy as jnp
from jax import lax
from jax.experimental import pallas as pl
from jax.experimental.pallas import tpu as pltpu
from jax.sharding import PartitionSpec as P

U = 64
R = 8
NB = 16
KL = 13
N1 = R + U
N2 = R + 2 * U
PACKED = R + U + U // 2
PITCH = 72
F32 = jnp.float32
BF16 = jnp.bfloat16
MESH = pl.DeviceIdType.MESH
NT = (((1,), (1,)), ((), ()))
NN = (((1,), (0,)), ((), ()))
LEVELS = (4, 8, 4)
CHUNKS = 4
ROWS = (0, 208, 416, 432, 448, 464)


def split(x):
    hi = x.astype(BF16)
    return hi, (x - hi.astype(F32)).astype(BF16)


def mm(a, b, dims):
    return lax.dot_general(a, b, dims, preferred_element_type=F32)


def dot3(x, w, dims=NN):
    m = x.shape[0]
    xh, xl = split(x)
    wh, wl = split(w)
    both = mm(jnp.concatenate([xh, xl], axis=0), wh, dims)
    return both[:m] + both[m:] + mm(xh, wl, dims)


def iota(shape, axis):
    return lax.broadcasted_iota(jnp.int32, shape, axis)


def lower_half():
    return iota((1, 128), 1) < U


def swap_halves(x):
    return pltpu.roll(x, U, axis=1)


def one_hot(lcols, ucols, active):
    e = iota((KL, 512), 0)
    group = iota((KL, 512), 1) // 16
    low = lcols[...].astype(F32).astype(BF16)
    up = ucols[...].astype(F32).astype(BF16)
    listed = mm(low, (group == e).astype(BF16), NN) + mm(up, (group == e + KL).astype(BF16), NN)
    lane = iota((1, 512), 1)
    k = lane % 16
    own = iota((NB, 512), 0) == iota((NB, 512), 1) % 16
    target = jnp.sum(jnp.where(own, listed, 0.0), axis=0, keepdims=True).astype(jnp.int32)
    target = jnp.where(lane >= ROWS[2], k, target)
    target = jnp.where(lane >= ROWS[3], 16, target)
    target = jnp.where(lane >= ROWS[4], 17, target)
    diag = (lane >= ROWS[2]) & (lane < ROWS[3])
    target = jnp.where((lane < ROWS[5]) & (diag | (k < active)), target, -1)
    r = iota((288, 512), 0)
    second = (r >= 144).astype(jnp.int32)
    column = 2 * (r // 16) - 17 * second
    return jnp.where((column == target) & (k == r % 16), 1.0, 0.0).astype(BF16)


def assemble(sources, lcols, ucols, active, stack, panel, sems):
    width = U * U // CHUNKS
    copies = []
    for q in range(CHUNKS):
        lanes = pl.ds(width * q, width)
        row = []
        for n, src in enumerate(sources):
            copy = pltpu.make_async_copy(
                src.at[:, lanes], stack.at[pl.ds(ROWS[n], ROWS[n + 1] - ROWS[n]), lanes], sems.at[n, q]
            )
            copy.start()
            row.append(copy)
        copies.append(row)
    stack[pl.ds(ROWS[5], 512 - ROWS[5]), :] = jnp.zeros((512 - ROWS[5], U * U), BF16)
    hot = one_hot(lcols, ucols, active)
    low = lower_half()
    tiles = 16 // CHUNKS
    for t in range(16):
        if t % tiles == 0:
            for copy in copies[t // tiles]:
                copy.wait()
        tile = mm(hot, stack[:, pl.ds(256 * t, 256)], NN)
        for s in range(2):
            even = tile[0:144, 128 * s : 128 * s + 128]
            odd = tile[144:288, 128 * s : 128 * s + 128]
            i = 4 * t + 2 * s
            panel[pl.ds(i, 144, stride=PITCH), :] = jnp.where(low, even, swap_halves(odd))
            panel[pl.ds(i + 1, 144, stride=PITCH), :] = jnp.where(low, swap_halves(even), odd)


def block(panel, c2, k):
    return panel[pl.ds((c2 * 16 + k) * PITCH, U), :]


def column_blocks(panel, c2, first, last):
    return jnp.concatenate([block(panel, c2, k) for k in range(first, last)], axis=0)


def pair_operator(panel, c):
    low = lower_half()
    zeros = jnp.zeros((U, 128), F32)
    even, odd = block(panel, c, 2 * c), block(panel, c, 2 * c + 1)
    right = jnp.where(low, 0.0, odd)
    inner = dot3(jnp.where(low, even, 0.0), jnp.concatenate([jnp.where(low, 0.0, even), zeros], axis=0))
    inner = dot3(inner, jnp.concatenate([zeros, right], axis=0))
    return jnp.concatenate([jnp.where(low, even, -inner), right], axis=0)


def forward(rhs, active, panel, work, gt, hacc, ops):
    live = (iota((1, NB * U), 1) // U) < active
    low = lower_half()
    eye = (iota((128, 128), 0) == iota((128, 128), 1)).astype(BF16)
    seeds = -mm(eye, column_blocks(panel, 8, 0, NB).astype(BF16), NT)
    work[0:R, :] = jnp.where(live, rhs[...], 0.0)
    work[R:, :] = seeds
    for c in range(8):
        ops[pl.ds(128 * c, 128), :] = pair_operator(panel, c)
    hacc[...] = jnp.where(iota((U, NB * U), 0) == iota((U, NB * U), 1), 1.0, 0.0)
    zeros = jnp.zeros((U, 128), F32)
    last = jnp.zeros((N1, 128), F32)
    for c in range(8):
        here = pl.ds(128 * c, 128)
        w = work[0:N1, here]
        inner = jnp.concatenate([zeros, jnp.where(low, block(panel, c, 2 * c + 1), 0.0)], axis=0)
        x = w - dot3(w, inner, NT)
        work[0:N1, here] = x
        g = dot3(hacc[:, here], ops[here, :])
        gt[:, here] = g
        mine = 2 * c + jnp.where(low, 0, 1) == active - 1
        last = last + jnp.where(mine, x, 0.0)
        if c < 7:
            rest = pl.ds(128 * (c + 1), 128 * (7 - c))
            work[0:N1, rest] -= dot3(x, column_blocks(panel, c, 2 * c + 2, NB), NT)
            weights = [column_blocks(panel, d, 2 * c, 2 * c + 2) for d in range(c + 1, 8)]
            hacc[:, rest] -= dot3(g, jnp.concatenate(weights, axis=1))
    boundary = last + swap_halves(last)
    weights = jnp.concatenate([jnp.zeros((U, NB * U), F32), gt[...]], axis=0)
    z0 = dot3(work[...], weights, NT)
    return jnp.concatenate([jnp.where(low, boundary, z0[:N1]), z0[N1:]], axis=0)


def backward_step(c, panel, work, zbuf, ops):
    here = pl.ds(128 * c, 128)
    z = dot3(work[:, here], ops[here, :], NT)
    zbuf[:, here] = z
    if c:
        work[:, pl.ds(0, 128 * c)] -= dot3(z, column_blocks(panel, c, 0, 2 * c), NT)


def unpack(m):
    low = lower_half()
    d = m[N1:]
    return jnp.concatenate(
        [m[:N1], jnp.where(low, 0.0, swap_halves(d)), jnp.where(low, 0.0, d)], axis=0
    )


def pack(m):
    top, bottom = m[N1 : N1 + U // 2], m[N1 + U // 2 :]
    return jnp.concatenate([m[:N1], jnp.where(lower_half(), swap_halves(top), bottom)], axis=0)


def compose(left, right):
    t = dot3(left[:N1, :U], right[R:N1])
    t = jnp.concatenate([t[:R] + right[:R], t[R:]], axis=0)
    weights = jnp.concatenate([jnp.zeros((U, 128), F32), left[N1:]], axis=0)
    s = dot3(jnp.concatenate([t, right[N1:]], axis=0), weights)
    return jnp.concatenate([jnp.where(lower_half(), t, s[:N1] + left[:N1]), s[N1:]], axis=0)


def identity_map():
    r = iota((N2, 128), 0)
    lane = iota((N2, 128), 1)
    one = ((r >= R) & (r < N1) & (lane == r - R)) | ((r >= N1) & (lane == r - N1 + U))
    return jnp.where(one, 1.0, 0.0)


def narrow(right, sibling, before, after):
    c = compose(jnp.where(right, sibling, after), jnp.where(right, before, sibling))
    return jnp.where(right, c, before), jnp.where(right, after, c)


def kernel(
    levels, rhs, lower, upper, diag, llow, lup, lcols, ucols, counts, *rest
):
    if levels is None:
        maps, zout, stack, panel, work, zbuf, gt, hacc, ops, in_sems = rest
        active = counts[0]
        assemble((lower, upper, diag, llow, lup), lcols, ucols, active, stack, panel, in_sems)
        maps[...] = pack(forward(rhs, active, panel, work, gt, hacc, ops))
        for c in reversed(range(8)):
            backward_step(c, panel, work, zout, ops)
        return
    (
        out, stack, panel, work, zbuf, gt, hacc, ops, in_sems,
        b_core, b_y, b_z, b_x, y_pairs, z_pairs, z_quads, sides,
        s_core, r_core, s_y, r_y, s_z, r_z, s_x, r_x,
    ) = rest
    nx, nz, ny = levels
    chain = lax.axis_index("chain")
    side = lax.axis_index("side")
    y = chain % ny
    zz = (chain // ny) % nz
    x = chain // (ny * nz)

    def at_core(k):
        return (chain, 1 - side)

    def at_y(k):
        return (chain - y + (y + k) % ny, side)

    def at_z(k):
        return (chain - zz * ny + ((zz + k) % nz) * ny, side)

    def at_x(k):
        return (((x + k) % nx) * (ny * nz) + chain % (ny * nz), side)

    peers = [at_core(1)]
    peers += [at_y(k) for k in range(1, ny)]
    peers += [at_z(k) for k in range(1, nz)]
    peers += [at_x(k) for k in range(1, nx)]
    barrier = pltpu.get_barrier_semaphore()
    for peer in peers:
        pl.semaphore_signal(barrier, inc=1, device_id=peer, device_id_type=MESH)

    def copies_of(buf, index, count, peer_of, send, recv):
        order = sorted(range(1, count), key=lambda k: min(k, count - k))
        return [
            pltpu.make_async_remote_copy(
                src_ref=buf.at[index],
                dst_ref=buf.at[index],
                send_sem=send.at[k - 1],
                recv_sem=recv.at[k - 1],
                device_id=peer_of(k),
                device_id_type=MESH,
            )
            for k in order
        ]

    def start(copies):
        for copy in copies:
            copy.start()

    def wait(copies):
        for copy in copies:
            copy.wait()

    fence = pl.when(chain >= 0)
    active = counts[0]
    assemble((lower, upper, diag, llow, lup), lcols, ucols, active, stack, panel, in_sems)
    b_core[side] = pack(forward(rhs, active, panel, work, gt, hacc, ops))
    pl.semaphore_wait(barrier, len(peers))

    core = copies_of(b_core, side, 2, at_core, s_core, r_core)
    start(core)
    wait(core)

    @fence
    def _():
        b_y[y] = pack(compose(unpack(b_core[0]), unpack(b_core[1])))

    ys = copies_of(b_y, y, ny, at_y, s_y, r_y)
    start(ys)

    @fence
    def _():
        for c in (7, 6, 5):
            backward_step(c, panel, work, zbuf, ops)

    wait(ys)

    @fence
    def _():
        nodes = [compose(unpack(b_y[i]), unpack(b_y[i + 1])) for i in range(0, ny, 2)]
        for i, node in enumerate(nodes):
            y_pairs[i] = node
        b_z[zz] = pack(compose(*nodes))

    zs = copies_of(b_z, zz, nz, at_z, s_z, r_z)
    start(zs)

    @fence
    def _():
        for c in (4, 3, 2, 1, 0):
            backward_step(c, panel, work, zbuf, ops)

    @fence
    def _():
        before = after = identity_map()
        before, after = narrow(side == 1, unpack(b_core[1 - side]), before, after)
        before, after = narrow(y % 2 == 1, unpack(b_y[y + 1 - 2 * (y % 2)]), before, after)
        before, after = narrow(y // 2 == 1, y_pairs[1 - y // 2], before, after)
        sides[0] = before
        sides[1] = after

    wait(zs)

    @fence
    def _():
        nodes = [compose(unpack(b_z[i]), unpack(b_z[i + 1])) for i in range(0, nz, 2)]
        for i, node in enumerate(nodes):
            z_pairs[i] = node
        nodes = [compose(nodes[i], nodes[i + 1]) for i in range(0, nz // 2, 2)]
        for i, node in enumerate(nodes):
            z_quads[i] = node
        b_x[x] = pack(compose(*nodes))

    xs = copies_of(b_x, x, nx, at_x, s_x, r_x)
    start(xs)

    @fence
    def _():
        before, after = sides[0], sides[1]
        before, after = narrow(zz % 2 == 1, unpack(b_z[zz + 1 - 2 * (zz % 2)]), before, after)
        pair = zz // 2
        before, after = narrow(pair % 2 == 1, z_pairs[pair + 1 - 2 * (pair % 2)], before, after)
        before, after = narrow(zz // 4 == 1, z_quads[1 - zz // 4], before, after)
        sides[0] = before
        sides[1] = after

    wait(xs)

    t = b_x[0, 0:R]
    p = jnp.zeros((R, U), F32)
    ends = [t]
    for j in range(1, nx):
        p = jnp.where(x == j, t[:, :U], p)
        t = dot3(t[:, :U], b_x[j, R:N1]) + b_x[j, 0:R]
        ends.append(t)
    q_run = ends[nx - 1][:, U:]
    q = jnp.zeros((R, U), F32)
    for j in reversed(range(nx - 1)):
        q = jnp.where(x == j, q_run, q)
        if j:
            q_run = dot3(q_run, unpack(b_x[j])[N1:, U:]) + ends[j][:, U:]
    own = unpack(b_core[side])
    before, after = sides[0], sides[1]
    p = dot3(p, before[R:N1, :U]) + before[:R, :U]
    t = dot3(p, own[R:N1, :U]) + own[:R, :U]
    t = dot3(t, after[R:N1]) + after[:R]
    q = t[:, U:] + dot3(q, after[N1:, U:])
    out[...] = zbuf[0:R, :] + dot3(jnp.concatenate([p, q], axis=1), zbuf[R:, :])


def local(levels, interpret, rhs, lower, lcols, upper, ucols, diag, llow, lup, counts):
    vmem = pl.BlockSpec(memory_space=pltpu.VMEM)
    anywhere = pl.BlockSpec(memory_space=pl.ANY)
    dma = pltpu.SemaphoreType.DMA
    flat = NB * KL
    lower = jnp.transpose(lower, (1, 0, 2)).reshape(flat, U * U)
    upper = jnp.transpose(upper, (1, 0, 2)).reshape(flat, U * U)
    cols = NB * U
    scratch = [
        pltpu.VMEM((512, U * U), BF16),
        pltpu.VMEM((144 * PITCH, 128), F32),
        pltpu.VMEM((N2, cols), F32),
        pltpu.VMEM((N2, cols), F32),
        pltpu.VMEM((U, cols), F32),
        pltpu.VMEM((U, cols), F32),
        pltpu.VMEM((cols, 128), F32),
        dma((5, CHUNKS)),
    ]
    if levels is None:
        outs = (jax.ShapeDtypeStruct((PACKED, 128), F32), jax.ShapeDtypeStruct((N2, cols), F32))
        params = pltpu.CompilerParams(vmem_limit_bytes=56 * 1024 * 1024)
    else:
        nx, nz, ny = levels
        outs = jax.ShapeDtypeStruct((R, cols), F32)
        scratch += [pltpu.VMEM((n, PACKED, 128), F32) for n in (2, ny, nz, nx)]
        scratch += [pltpu.VMEM((n, N2, 128), F32) for n in (ny // 2, nz // 2, nz // 4, 2)]
        scratch += [dma((n - 1,)) for n in (2, 2, ny, ny, nz, nz, nx, nx)]
        params = pltpu.CompilerParams(
            collective_id=0, has_side_effects=True, vmem_limit_bytes=56 * 1024 * 1024
        )
    return pl.pallas_call(
        functools.partial(kernel, levels),
        out_shape=outs,
        in_specs=[vmem] + [anywhere] * 5 + [vmem] * 2 + [pl.BlockSpec(memory_space=pltpu.SMEM)],
        out_specs=jax.tree.map(lambda _: vmem, outs),
        scratch_shapes=scratch,
        compiler_params=params,
        interpret=interpret,
        name="ilu_apply",
    )(rhs, lower, upper, diag, llow, lup, lcols, ucols, counts)


def solution(mesh, levels=LEVELS):
    both = ("chain", "side")
    return jax.shard_map(
        functools.partial(local, levels, False),
        mesh=mesh,
        in_specs=(
            P(None, both),
            P(both, None, None),
            P(both, None),
            P(both, None, None),
            P(both, None),
            P(both, None),
            P(both, None),
            P(both, None),
            P(both),
        ),
        out_specs=P(None, both),
        check_vma=False,
    )
```

```python
import functools

import jax
import jax.numpy as jnp
from jax import lax
from jax.experimental import pallas as pl
from jax.experimental.pallas import tpu as pltpu
from jax.sharding import PartitionSpec as P

U = 64
R = 8
NB = 16
KL = 13
N1 = R + U
N2 = R + 2 * U
PACKED = R + U + U // 2
PITCH = 72
HALF = 56
F32 = jnp.float32
BF16 = jnp.bfloat16
MESH = pl.DeviceIdType.MESH
NT = (((1,), (1,)), ((), ()))
NN = (((1,), (0,)), ((), ()))
LEVELS = (4, 8, 4)
CHUNKS = 4
ROWS = (0, 208, 416, 432, 448, 464)


def split(x):
    hi = x.astype(BF16)
    return hi, (x - hi.astype(F32)).astype(BF16)


def mm(a, b, dims):
    return lax.dot_general(a, b, dims, preferred_element_type=F32)


def dot3(x, w, dims=NN):
    m = x.shape[0]
    xh, xl = split(x)
    wh, wl = split(w)
    both = mm(jnp.concatenate([xh, xl], axis=0), wh, dims)
    return both[:m] + both[m:] + mm(xh, wl, dims)


def iota(shape, axis):
    return lax.broadcasted_iota(jnp.int32, shape, axis)


def lower_half():
    return iota((1, 128), 1) < U


def swap_halves(x):
    return pltpu.roll(x, U, axis=1)


def one_hot(lcols, ucols, active):
    e = iota((KL, 512), 0)
    group = iota((KL, 512), 1) // 16
    low = lcols[...].astype(F32).astype(BF16)
    up = ucols[...].astype(F32).astype(BF16)
    listed = mm(low, (group == e).astype(BF16), NN) + mm(up, (group == e + KL).astype(BF16), NN)
    lane = iota((1, 512), 1)
    k = lane % 16
    own = iota((NB, 512), 0) == iota((NB, 512), 1) % 16
    target = jnp.sum(jnp.where(own, listed, 0.0), axis=0, keepdims=True).astype(jnp.int32)
    target = jnp.where(lane >= ROWS[2], k, target)
    target = jnp.where(lane >= ROWS[3], 16, target)
    target = jnp.where(lane >= ROWS[4], 17, target)
    diag = (lane >= ROWS[2]) & (lane < ROWS[3])
    target = jnp.where((lane < ROWS[5]) & (diag | (k < active)), target, -1)
    r = iota((288, 512), 0)
    second = (r >= 144).astype(jnp.int32)
    column = 2 * (r // 16) - 17 * second
    return jnp.where((column == target) & (k == r % 16), 1.0, 0.0).astype(BF16)


def assemble(sources, lcols, ucols, active, stack, panel, sems):
    width = U * U // CHUNKS
    copies = []
    for q in range(CHUNKS):
        lanes = pl.ds(width * q, width)
        row = []
        for n, src in enumerate(sources):
            copy = pltpu.make_async_copy(
                src.at[:, lanes], stack.at[pl.ds(ROWS[n], ROWS[n + 1] - ROWS[n]), lanes], sems.at[n, q]
            )
            copy.start()
            row.append(copy)
        copies.append(row)
    stack[pl.ds(ROWS[5], 512 - ROWS[5]), :] = jnp.zeros((512 - ROWS[5], U * U), BF16)
    hot = one_hot(lcols, ucols, active)
    low = lower_half()
    tiles = 16 // CHUNKS
    for t in range(16):
        if t % tiles == 0:
            for copy in copies[t // tiles]:
                copy.wait()
        tile = mm(hot, stack[:, pl.ds(256 * t, 256)], NN)
        for s in range(2):
            even = tile[0:144, 128 * s : 128 * s + 128]
            odd = tile[144:288, 128 * s : 128 * s + 128]
            i = 4 * t + 2 * s
            panel[pl.ds(i, 144, stride=PITCH), :] = jnp.where(low, even, swap_halves(odd))
            panel[pl.ds(i + 1, 144, stride=PITCH), :] = jnp.where(low, swap_halves(even), odd)


def block(panel, c2, k):
    return panel[pl.ds((c2 * 16 + k) * PITCH, U), :]


def column_blocks(panel, c2, first, last):
    return jnp.concatenate([block(panel, c2, k) for k in range(first, last)], axis=0)


def pair_operator(panel, c):
    low = lower_half()
    zeros = jnp.zeros((U, 128), F32)
    even, odd = block(panel, c, 2 * c), block(panel, c, 2 * c + 1)
    right = jnp.where(low, 0.0, odd)
    inner = dot3(jnp.where(low, even, 0.0), jnp.concatenate([jnp.where(low, 0.0, even), zeros], axis=0))
    inner = dot3(inner, jnp.concatenate([zeros, right], axis=0))
    return jnp.concatenate([jnp.where(low, even, -inner), right], axis=0)


def forward(rhs, active, panel, work, gt, hacc, ops):
    live = (iota((1, NB * U), 1) // U) < active
    low = lower_half()
    eye = (iota((128, 128), 0) == iota((128, 128), 1)).astype(BF16)
    seeds = -mm(eye, column_blocks(panel, 8, 0, NB).astype(BF16), NT)
    work[0:R, :] = jnp.where(live, rhs[...], 0.0)
    work[R:, :] = seeds
    for c in range(8):
        ops[pl.ds(128 * c, 128), :] = pair_operator(panel, c)
    hacc[...] = jnp.where(iota((U, NB * U), 0) == iota((U, NB * U), 1), 1.0, 0.0)
    zeros = jnp.zeros((U, 128), F32)
    last = jnp.zeros((N1, 128), F32)
    for c in range(8):
        here = pl.ds(128 * c, 128)
        w = work[0:N1, here]
        inner = jnp.concatenate([zeros, jnp.where(low, block(panel, c, 2 * c + 1), 0.0)], axis=0)
        x = w - dot3(w, inner, NT)
        work[0:N1, here] = x
        g = dot3(hacc[:, here], ops[here, :])
        gt[:, here] = g
        mine = 2 * c + jnp.where(low, 0, 1) == active - 1
        last = last + jnp.where(mine, x, 0.0)
        if c < 7:
            rest = pl.ds(128 * (c + 1), 128 * (7 - c))
            work[0:N1, rest] -= dot3(x, column_blocks(panel, c, 2 * c + 2, NB), NT)
            weights = [column_blocks(panel, d, 2 * c, 2 * c + 2) for d in range(c + 1, 8)]
            hacc[:, rest] -= dot3(g, jnp.concatenate(weights, axis=1))
    boundary = last + swap_halves(last)
    weights = jnp.concatenate([jnp.zeros((U, NB * U), F32), gt[...]], axis=0)
    z0 = dot3(work[...], weights, NT)
    return jnp.concatenate([jnp.where(low, boundary, z0[:N1]), z0[N1:]], axis=0)


def backward_step(c, panel, work, zbuf, ops):
    here = pl.ds(128 * c, 128)
    z = dot3(work[:, here], ops[here, :], NT)
    zbuf[:, here] = z
    if c:
        work[:, pl.ds(0, 128 * c)] -= dot3(z, column_blocks(panel, c, 0, 2 * c), NT)


def unpack(m):
    low = lower_half()
    d = m[N1:]
    return jnp.concatenate(
        [m[:N1], jnp.where(low, 0.0, swap_halves(d)), jnp.where(low, 0.0, d)], axis=0
    )


def pack(m):
    top, bottom = m[N1 : N1 + U // 2], m[N1 + U // 2 :]
    return jnp.concatenate([m[:N1], jnp.where(lower_half(), swap_halves(top), bottom)], axis=0)


def compose(left, right):
    t = dot3(left[:N1, :U], right[R:N1])
    t = jnp.concatenate([t[:R] + right[:R], t[R:]], axis=0)
    weights = jnp.concatenate([jnp.zeros((U, 128), F32), left[N1:]], axis=0)
    s = dot3(jnp.concatenate([t, right[N1:]], axis=0), weights)
    return jnp.concatenate([jnp.where(lower_half(), t, s[:N1] + left[:N1]), s[N1:]], axis=0)


def identity_map():
    r = iota((N2, 128), 0)
    lane = iota((N2, 128), 1)
    one = ((r >= R) & (r < N1) & (lane == r - R)) | ((r >= N1) & (lane == r - N1 + U))
    return jnp.where(one, 1.0, 0.0)


def narrow(right, sibling, before, after):
    c = compose(jnp.where(right, sibling, after), jnp.where(right, before, sibling))
    return jnp.where(right, c, before), jnp.where(right, after, c)


def kernel(
    levels, rhs, lower, upper, diag, llow, lup, lcols, ucols, counts, *rest
):
    if levels is None:
        maps, zout, stack, panel, work, zbuf, gt, hacc, ops, in_sems = rest
        active = counts[0]
        assemble((lower, upper, diag, llow, lup), lcols, ucols, active, stack, panel, in_sems)
        maps[...] = pack(forward(rhs, active, panel, work, gt, hacc, ops))
        for c in reversed(range(8)):
            backward_step(c, panel, work, zout, ops)
        return
    (
        out, stack, panel, work, zbuf, gt, hacc, ops, in_sems,
        b_core, b_y, b_z, b_x, y_pairs, z_pairs, z_quads, sides,
        s_core, r_core, s_y, r_y, s_z, r_z, s_x, r_x, s_f, r_f,
    ) = rest
    nx, nz, ny = levels
    chain = lax.axis_index("chain")
    side = lax.axis_index("side")
    y = chain % ny
    zz = (chain // ny) % nz
    x = chain // (ny * nz)

    def at_core(k):
        return (chain, 1 - side)

    def at_y(k):
        return (chain - y + (y + k) % ny, side)

    def at_z(k):
        return (chain - zz * ny + ((zz + k) % nz) * ny, side)

    def at_x(k):
        return (((x + k) % nx) * (ny * nz) + chain % (ny * nz), side)

    peers = [at_core(1)]
    peers += [at_y(k) for k in range(1, ny)]
    peers += [at_z(k) for k in range(1, nz)]
    peers += [at_x(k) for k in range(1, nx)]
    barrier = pltpu.get_barrier_semaphore()
    for peer in peers:
        pl.semaphore_signal(barrier, inc=1, device_id=peer, device_id_type=MESH)

    def remote(src, dst, send, recv, peer):
        return pltpu.make_async_remote_copy(
            src_ref=src, dst_ref=dst, send_sem=send, recv_sem=recv, device_id=peer, device_id_type=MESH
        )

    def copies_of(buf, index, count, peer_of, send, recv):
        order = sorted(range(1, count), key=lambda k: min(k, count - k))
        return [
            remote(buf.at[index], buf.at[index], send.at[k - 1], recv.at[k - 1], peer_of(k)) for k in order
        ]

    def start(copies):
        for copy in copies:
            copy.start()

    def wait(copies):
        for copy in copies:
            copy.wait()

    fence = pl.when(chain >= 0)
    active = counts[0]
    assemble((lower, upper, diag, llow, lup), lcols, ucols, active, stack, panel, in_sems)
    b_core[side] = pack(forward(rhs, active, panel, work, gt, hacc, ops))
    pl.semaphore_wait(barrier, len(peers))

    core = copies_of(b_core, side, 2, at_core, s_core, r_core)
    start(core)
    wait(core)

    @fence
    def _():
        b_y[y] = pack(compose(unpack(b_core[0]), unpack(b_core[1])))

    ys = copies_of(b_y, y, ny, at_y, s_y, r_y)
    start(ys)

    @fence
    def _():
        for c in (7, 6, 5):
            backward_step(c, panel, work, zbuf, ops)

    wait(ys)

    @fence
    def _():
        nodes = [compose(unpack(b_y[i]), unpack(b_y[i + 1])) for i in range(0, ny, 2)]
        for i, node in enumerate(nodes):
            y_pairs[i] = node
        b_z[zz, 0:PACKED] = pack(compose(*nodes))
        b_z[zz, PACKED:] = jnp.zeros((2 * HALF - PACKED, 128), F32)

    mine = pl.ds(pl.multiple_of(side * HALF, 8), HALF)
    order = sorted(range(1, nz), key=lambda k: min(k, nz - k))
    zs, forwards = [], []
    for k in order:
        part = b_z.at[zz, mine]
        zs.append(remote(part, part, s_z.at[k - 1], r_z.at[k - 1], at_z(k)))
        part = b_z.at[(zz + nz - k) % nz, mine]
        forwards.append(remote(part, part, s_f.at[k - 1], r_f.at[k - 1], at_core(1)))
    start(zs)

    @fence
    def _():
        for c in (4, 3, 2, 1, 0):
            backward_step(c, panel, work, zbuf, ops)

    @fence
    def _():
        before = after = identity_map()
        before, after = narrow(side == 1, unpack(b_core[1 - side]), before, after)
        before, after = narrow(y % 2 == 1, unpack(b_y[y + 1 - 2 * (y % 2)]), before, after)
        before, after = narrow(y // 2 == 1, y_pairs[1 - y // 2], before, after)
        sides[0] = before
        sides[1] = after

    for arriving, forward_copy in zip(zs, forwards):
        arriving.wait_recv()
        forward_copy.start()
    for arriving in zs:
        arriving.wait_send()
    wait(forwards)

    @fence
    def _():
        nodes = [compose(unpack(b_z[i, 0:PACKED]), unpack(b_z[i + 1, 0:PACKED])) for i in range(0, nz, 2)]
        for i, node in enumerate(nodes):
            z_pairs[i] = node
        nodes = [compose(nodes[i], nodes[i + 1]) for i in range(0, nz // 2, 2)]
        for i, node in enumerate(nodes):
            z_quads[i] = node
        b_x[x] = pack(compose(*nodes))

    xs = copies_of(b_x, x, nx, at_x, s_x, r_x)
    start(xs)

    @fence
    def _():
        before, after = sides[0], sides[1]
        before, after = narrow(zz % 2 == 1, unpack(b_z[zz + 1 - 2 * (zz % 2), 0:PACKED]), before, after)
        pair = zz // 2
        before, after = narrow(pair % 2 == 1, z_pairs[pair + 1 - 2 * (pair % 2)], before, after)
        before, after = narrow(zz // 4 == 1, z_quads[1 - zz // 4], before, after)
        sides[0] = before
        sides[1] = after

    wait(xs)

    t = b_x[0, 0:R]
    p = jnp.zeros((R, U), F32)
    ends = [t]
    for j in range(1, nx):
        p = jnp.where(x == j, t[:, :U], p)
        t = dot3(t[:, :U], b_x[j, R:N1]) + b_x[j, 0:R]
        ends.append(t)
    q_run = ends[nx - 1][:, U:]
    q = jnp.zeros((R, U), F32)
    for j in reversed(range(nx - 1)):
        q = jnp.where(x == j, q_run, q)
        if j:
            q_run = dot3(q_run, unpack(b_x[j])[N1:, U:]) + ends[j][:, U:]
    own = unpack(b_core[side])
    before, after = sides[0], sides[1]
    p = dot3(p, before[R:N1, :U]) + before[:R, :U]
    t = dot3(p, own[R:N1, :U]) + own[:R, :U]
    t = dot3(t, after[R:N1]) + after[:R]
    q = t[:, U:] + dot3(q, after[N1:, U:])
    out[...] = zbuf[0:R, :] + dot3(jnp.concatenate([p, q], axis=1), zbuf[R:, :])


def local(levels, interpret, rhs, lower, lcols, upper, ucols, diag, llow, lup, counts):
    vmem = pl.BlockSpec(memory_space=pltpu.VMEM)
    anywhere = pl.BlockSpec(memory_space=pl.ANY)
    dma = pltpu.SemaphoreType.DMA
    flat = NB * KL
    lower = jnp.transpose(lower, (1, 0, 2)).reshape(flat, U * U)
    upper = jnp.transpose(upper, (1, 0, 2)).reshape(flat, U * U)
    cols = NB * U
    scratch = [
        pltpu.VMEM((512, U * U), BF16),
        pltpu.VMEM((144 * PITCH, 128), F32),
        pltpu.VMEM((N2, cols), F32),
        pltpu.VMEM((N2, cols), F32),
        pltpu.VMEM((U, cols), F32),
        pltpu.VMEM((U, cols), F32),
        pltpu.VMEM((cols, 128), F32),
        dma((5, CHUNKS)),
    ]
    if levels is None:
        outs = (jax.ShapeDtypeStruct((PACKED, 128), F32), jax.ShapeDtypeStruct((N2, cols), F32))
        params = pltpu.CompilerParams(vmem_limit_bytes=56420000)
    else:
        nx, nz, ny = levels
        outs = jax.ShapeDtypeStruct((R, cols), F32)
        scratch += [pltpu.VMEM((n, m, 128), F32) for n, m in ((2, PACKED), (ny, PACKED), (nz, 2 * HALF), (nx, PACKED))]
        scratch += [pltpu.VMEM((n, N2, 128), F32) for n in (ny // 2, nz // 2, nz // 4, 2)]
        scratch += [dma((n - 1,)) for n in (2, 2, ny, ny, nz, nz, nx, nx, nz, nz)]
        params = pltpu.CompilerParams(
            collective_id=0, has_side_effects=True, vmem_limit_bytes=56420000
        )
    return pl.pallas_call(
        functools.partial(kernel, levels),
        out_shape=outs,
        in_specs=[vmem] + [anywhere] * 5 + [vmem] * 2 + [pl.BlockSpec(memory_space=pltpu.SMEM)],
        out_specs=jax.tree.map(lambda _: vmem, outs),
        scratch_shapes=scratch,
        compiler_params=params,
        interpret=interpret,
        name="ilu_apply",
    )(rhs, lower, upper, diag, llow, lup, lcols, ucols, counts)


def solution(mesh, levels=LEVELS):
    both = ("chain", "side")
    return jax.shard_map(
        functools.partial(local, levels, False),
        mesh=mesh,
        in_specs=(
            P(None, both),
            P(both, None, None),
            P(both, None),
            P(both, None, None),
            P(both, None),
            P(both, None),
            P(both, None),
            P(both, None),
            P(both),
        ),
        out_specs=P(None, both),
        check_vma=False,
    )
```

```python
import functools

import jax
import jax.numpy as jnp
from jax import lax
from jax.experimental import pallas as pl
from jax.experimental.pallas import tpu as pltpu
from jax.sharding import PartitionSpec as P

U = 64
R = 8
NB = 16
KL = 13
N1 = R + U
N2 = R + 2 * U
PACKED = R + U + U // 2
PITCH = 72
HALF = 56
F32 = jnp.float32
BF16 = jnp.bfloat16
MESH = pl.DeviceIdType.MESH
NT = (((1,), (1,)), ((), ()))
NN = (((1,), (0,)), ((), ()))
LEVELS = (4, 8, 4)
CHUNKS = 2
GROUPS = 2 * KL + 3


def split(x):
    hi = x.astype(BF16)
    return hi, (x - hi.astype(F32)).astype(BF16)


def mm(a, b, dims):
    return lax.dot_general(a, b, dims, preferred_element_type=F32)


def dot3(x, w, dims=NN):
    m = x.shape[0]
    xh, xl = split(x)
    wh, wl = split(w)
    both = mm(jnp.concatenate([xh, xl], axis=0), wh, dims)
    return both[:m] + both[m:] + mm(xh, wl, dims)


def iota(shape, axis):
    return lax.broadcasted_iota(jnp.int32, shape, axis)


def lower_half():
    return iota((1, 128), 1) < U


def swap_halves(x):
    return pltpu.roll(x, U, axis=1)


def one_hot(lcols, ucols, active, half):
    e = iota((KL, 256), 0)
    group = iota((KL, 256), 1) // 8
    low = lcols[...].astype(F32).astype(BF16)
    up = ucols[...].astype(F32).astype(BF16)
    listed = mm(low, (group == e).astype(BF16), NN) + mm(up, (group == e + KL).astype(BF16), NN)
    lane = iota((1, 256), 1)
    group = lane // 8
    k = lane % 8 + 8 * half
    own = iota((NB, 256), 0) == iota((NB, 256), 1) % 8 + 8 * half
    target = jnp.sum(jnp.where(own, listed, 0.0), axis=0, keepdims=True).astype(jnp.int32)
    target = jnp.where(group == 2 * KL, k, target)
    target = jnp.where(group == 2 * KL + 1, 16, target)
    target = jnp.where(group == 2 * KL + 2, 17, target)
    target = jnp.where((group < GROUPS) & ((group == 2 * KL) | (k < active)), target, -1)
    r = iota((144, 256), 0)
    second = (r >= 72).astype(jnp.int32)
    column = 2 * (r // 8) - 17 * second
    return jnp.where((column == target) & (lane % 8 == r % 8), 1.0, 0.0).astype(BF16)


def assemble(sources, few, lcols, ucols, active, stack, panel, sems):
    width = U * U // CHUNKS
    copies = {}
    for copy in few:
        copy.start()
    for half in range(2):
        for q in range(CHUNKS):
            lanes = pl.ds(width * q, width)
            row, first = [], 0
            for n, src in enumerate(sources):
                count = src.shape[0]
                copy = pltpu.make_async_copy(
                    src.at[:, pl.ds(8 * half, 8), lanes],
                    stack.at[half, pl.ds(first, count), :, lanes],
                    sems.at[n, half * CHUNKS + q],
                )
                copy.start()
                row.append(copy)
                first += count
            copies[half, q] = row
    stack[:, GROUPS:] = jnp.zeros((2, 32 - GROUPS, 8, U * U), BF16)
    low = lower_half()
    tiles = 16 // CHUNKS
    for copy in few:
        copy.wait()
    for half in range(2):
        hot = one_hot(lcols, ucols, active, half)
        for t in range(16):
            if t % tiles == 0:
                for copy in copies[half, t // tiles]:
                    copy.wait()
            rows = stack[half, :, :, pl.ds(256 * t, 256)].reshape(256, 256)
            tile = mm(hot, rows, NN)
            for s in range(2):
                even = tile[0:72, 128 * s : 128 * s + 128]
                odd = tile[72:144, 128 * s : 128 * s + 128]
                i = 4 * t + 2 * s
                first = jnp.where(low, even, swap_halves(odd))
                second = jnp.where(low, swap_halves(even), odd)
                for c2 in range(9):
                    base = (c2 * 16 + 8 * half) * PITCH + i
                    panel[pl.ds(base, 8, stride=PITCH), :] = first[8 * c2 : 8 * c2 + 8]
                    panel[pl.ds(base + 1, 8, stride=PITCH), :] = second[8 * c2 : 8 * c2 + 8]


def block(panel, c2, k):
    return panel[pl.ds((c2 * 16 + k) * PITCH, U), :]


def column_blocks(panel, c2, first, last):
    return jnp.concatenate([block(panel, c2, k) for k in range(first, last)], axis=0)


def pair_operator(panel, c):
    low = lower_half()
    zeros = jnp.zeros((U, 128), F32)
    even, odd = block(panel, c, 2 * c), block(panel, c, 2 * c + 1)
    right = jnp.where(low, 0.0, odd)
    inner = dot3(jnp.where(low, even, 0.0), jnp.concatenate([jnp.where(low, 0.0, even), zeros], axis=0))
    inner = dot3(inner, jnp.concatenate([zeros, right], axis=0))
    return jnp.concatenate([jnp.where(low, even, -inner), right], axis=0)


def forward(rhs, active, panel, work, gt, hacc, ops):
    live = (iota((1, NB * U), 1) // U) < active
    low = lower_half()
    eye = (iota((128, 128), 0) == iota((128, 128), 1)).astype(BF16)
    seeds = -mm(eye, column_blocks(panel, 8, 0, NB).astype(BF16), NT)
    work[0:R, :] = jnp.where(live, rhs[...], 0.0)
    work[R:, :] = seeds
    for c in range(8):
        ops[pl.ds(128 * c, 128), :] = pair_operator(panel, c)
    hacc[...] = jnp.where(iota((U, NB * U), 0) == iota((U, NB * U), 1), 1.0, 0.0)
    zeros = jnp.zeros((U, 128), F32)
    last = jnp.zeros((N1, 128), F32)
    for c in range(8):
        here = pl.ds(128 * c, 128)
        w = work[0:N1, here]
        inner = jnp.concatenate([zeros, jnp.where(low, block(panel, c, 2 * c + 1), 0.0)], axis=0)
        x = w - dot3(w, inner, NT)
        work[0:N1, here] = x
        g = dot3(hacc[:, here], ops[here, :])
        gt[:, here] = g
        mine = 2 * c + jnp.where(low, 0, 1) == active - 1
        last = last + jnp.where(mine, x, 0.0)
        if c < 7:
            rest = pl.ds(128 * (c + 1), 128 * (7 - c))
            work[0:N1, rest] -= dot3(x, column_blocks(panel, c, 2 * c + 2, NB), NT)
            weights = [column_blocks(panel, d, 2 * c, 2 * c + 2) for d in range(c + 1, 8)]
            hacc[:, rest] -= dot3(g, jnp.concatenate(weights, axis=1))
    boundary = last + swap_halves(last)
    weights = jnp.concatenate([jnp.zeros((U, NB * U), F32), gt[...]], axis=0)
    z0 = dot3(work[...], weights, NT)
    return jnp.concatenate([jnp.where(low, boundary, z0[:N1]), z0[N1:]], axis=0)


def backward_step(c, panel, work, zbuf, ops):
    here = pl.ds(128 * c, 128)
    z = dot3(work[:, here], ops[here, :], NT)
    zbuf[:, here] = z
    if c:
        work[:, pl.ds(0, 128 * c)] -= dot3(z, column_blocks(panel, c, 0, 2 * c), NT)


def unpack(m):
    low = lower_half()
    d = m[N1:]
    return jnp.concatenate(
        [m[:N1], jnp.where(low, 0.0, swap_halves(d)), jnp.where(low, 0.0, d)], axis=0
    )


def pack(m):
    top, bottom = m[N1 : N1 + U // 2], m[N1 + U // 2 :]
    return jnp.concatenate([m[:N1], jnp.where(lower_half(), swap_halves(top), bottom)], axis=0)


def compose(left, right):
    t = dot3(left[:N1, :U], right[R:N1])
    t = jnp.concatenate([t[:R] + right[:R], t[R:]], axis=0)
    weights = jnp.concatenate([jnp.zeros((U, 128), F32), left[N1:]], axis=0)
    s = dot3(jnp.concatenate([t, right[N1:]], axis=0), weights)
    return jnp.concatenate([jnp.where(lower_half(), t, s[:N1] + left[:N1]), s[N1:]], axis=0)


def identity_map():
    r = iota((N2, 128), 0)
    lane = iota((N2, 128), 1)
    one = ((r >= R) & (r < N1) & (lane == r - R)) | ((r >= N1) & (lane == r - N1 + U))
    return jnp.where(one, 1.0, 0.0)


def narrow(right, sibling, before, after):
    c = compose(jnp.where(right, sibling, after), jnp.where(right, before, sibling))
    return jnp.where(right, c, before), jnp.where(right, after, c)


def kernel(
    levels, rhs_in, lower, upper, diag, llow, lup, lcols_in, ucols_in, counts, *rest
):
    if levels is None:
        maps, zout, stack, panel, work, zbuf, gt, hacc, ops, in_sems, rhs, lcols, ucols, few_sems = rest
        few = [
            pltpu.make_async_copy(src, dst, few_sems.at[n])
            for n, (src, dst) in enumerate(((lcols_in, lcols), (ucols_in, ucols), (rhs_in, rhs)))
        ]
        active = counts[0]
        assemble((lower, upper, diag, llow, lup), few, lcols, ucols, active, stack, panel, in_sems)
        maps[...] = pack(forward(rhs, active, panel, work, gt, hacc, ops))
        for c in reversed(range(8)):
            backward_step(c, panel, work, zout, ops)
        return
    (
        out, stack, panel, work, zbuf, gt, hacc, ops, in_sems, rhs, lcols, ucols, few_sems,
        b_core, b_y, b_z, b_x, y_pairs, z_pairs, z_quads, sides,
        s_core, r_core, s_y, r_y, s_fy, r_fy, s_z, r_z, s_fz, r_fz, s_x, r_x, s_fx, r_fx,
    ) = rest
    nx, nz, ny = levels
    chain = lax.axis_index("chain")
    side = lax.axis_index("side")
    y = chain % ny
    zz = (chain // ny) % nz
    x = chain // (ny * nz)

    def at_core():
        return (chain, 1 - side)

    def at_y(k):
        return (chain - y + (y + k) % ny, side)

    def at_z(k):
        return (chain - zz * ny + ((zz + k) % nz) * ny, side)

    def at_x(k):
        return (((x + k) % nx) * (ny * nz) + chain % (ny * nz), side)

    peers = [at_core()]
    peers += [at_y(k) for k in range(1, ny)]
    peers += [at_z(k) for k in range(1, nz)]
    peers += [at_x(k) for k in range(1, nx)]
    barrier = pltpu.get_barrier_semaphore()
    for peer in peers:
        pl.semaphore_signal(barrier, inc=1, device_id=peer, device_id_type=MESH)

    def remote(src, dst, send, recv, peer):
        return pltpu.make_async_remote_copy(
            src_ref=src, dst_ref=dst, send_sem=send, recv_sem=recv, device_id=peer, device_id_type=MESH
        )

    mine = pl.ds(pl.multiple_of(side * HALF, 8), HALF)

    def put(buf, index, m):
        buf[index, 0:PACKED] = pack(m)
        buf[index, PACKED:] = jnp.zeros((2 * HALF - PACKED, 128), F32)

    def ring(buf, index, count, peer_of, send, recv, send_on, recv_on):
        arrivals, handovers = [], []
        for k in sorted(range(1, count), key=lambda k: min(k, count - k)):
            part = buf.at[index, mine]
            arrivals.append(remote(part, part, send.at[k - 1], recv.at[k - 1], peer_of(k)))
            part = buf.at[(index + count - k) % count, mine]
            handovers.append(remote(part, part, send_on.at[k - 1], recv_on.at[k - 1], at_core()))
        for copy in arrivals:
            copy.start()
        return arrivals, handovers

    def finish(copies):
        for arriving, handover in zip(*copies):
            arriving.wait_recv()
            handover.start()
        for arriving in copies[0]:
            arriving.wait_send()
        for handover in copies[1]:
            handover.wait()

    fence = pl.when(chain >= 0)
    few = [
        pltpu.make_async_copy(src, dst, few_sems.at[n])
        for n, (src, dst) in enumerate(((lcols_in, lcols), (ucols_in, ucols), (rhs_in, rhs)))
    ]
    active = counts[0]
    assemble((lower, upper, diag, llow, lup), few, lcols, ucols, active, stack, panel, in_sems)
    b_core[side] = pack(forward(rhs, active, panel, work, gt, hacc, ops))
    pl.semaphore_wait(barrier, len(peers))

    core = remote(b_core.at[side], b_core.at[side], s_core, r_core, at_core())
    core.start()
    core.wait()

    @fence
    def _():
        put(b_y, y, compose(unpack(b_core[0]), unpack(b_core[1])))

    ys = ring(b_y, y, ny, at_y, s_y, r_y, s_fy, r_fy)

    @fence
    def _():
        for c in (7, 6, 5):
            backward_step(c, panel, work, zbuf, ops)

    finish(ys)

    @fence
    def _():
        nodes = [compose(unpack(b_y[i, 0:PACKED]), unpack(b_y[i + 1, 0:PACKED])) for i in range(0, ny, 2)]
        for i, node in enumerate(nodes):
            y_pairs[i] = node
        put(b_z, zz, compose(*nodes))

    zs = ring(b_z, zz, nz, at_z, s_z, r_z, s_fz, r_fz)

    @fence
    def _():
        for c in (4, 3, 2, 1, 0):
            backward_step(c, panel, work, zbuf, ops)

    @fence
    def _():
        before = after = identity_map()
        before, after = narrow(side == 1, unpack(b_core[1 - side]), before, after)
        before, after = narrow(y % 2 == 1, unpack(b_y[y + 1 - 2 * (y % 2), 0:PACKED]), before, after)
        before, after = narrow(y // 2 == 1, y_pairs[1 - y // 2], before, after)
        sides[0] = before
        sides[1] = after

    finish(zs)

    @fence
    def _():
        nodes = [compose(unpack(b_z[i, 0:PACKED]), unpack(b_z[i + 1, 0:PACKED])) for i in range(0, nz, 2)]
        for i, node in enumerate(nodes):
            z_pairs[i] = node
        nodes = [compose(nodes[i], nodes[i + 1]) for i in range(0, nz // 2, 2)]
        for i, node in enumerate(nodes):
            z_quads[i] = node
        put(b_x, x, compose(*nodes))

    xs = ring(b_x, x, nx, at_x, s_x, r_x, s_fx, r_fx)

    @fence
    def _():
        before, after = sides[0], sides[1]
        before, after = narrow(zz % 2 == 1, unpack(b_z[zz + 1 - 2 * (zz % 2), 0:PACKED]), before, after)
        pair = zz // 2
        before, after = narrow(pair % 2 == 1, z_pairs[pair + 1 - 2 * (pair % 2)], before, after)
        before, after = narrow(zz // 4 == 1, z_quads[1 - zz // 4], before, after)
        sides[0] = before
        sides[1] = after

    finish(xs)

    t = b_x[0, 0:R]
    p = jnp.zeros((R, U), F32)
    ends = [t]
    for j in range(1, nx):
        p = jnp.where(x == j, t[:, :U], p)
        t = dot3(t[:, :U], b_x[j, R:N1]) + b_x[j, 0:R]
        ends.append(t)
    q_run = ends[nx - 1][:, U:]
    q = jnp.zeros((R, U), F32)
    for j in reversed(range(nx - 1)):
        q = jnp.where(x == j, q_run, q)
        if j:
            q_run = dot3(q_run, unpack(b_x[j, 0:PACKED])[N1:, U:]) + ends[j][:, U:]
    own = unpack(b_core[side])
    before, after = sides[0], sides[1]
    p = dot3(p, before[R:N1, :U]) + before[:R, :U]
    t = dot3(p, own[R:N1, :U]) + own[:R, :U]
    t = dot3(t, after[R:N1]) + after[:R]
    q = t[:, U:] + dot3(q, after[N1:, U:])
    out[...] = zbuf[0:R, :] + dot3(jnp.concatenate([p, q], axis=1), zbuf[R:, :])


def local(levels, interpret, rhs, lower, lcols, upper, ucols, diag, llow, lup, counts):
    vmem = pl.BlockSpec(memory_space=pltpu.VMEM)
    anywhere = pl.BlockSpec(memory_space=pl.ANY)
    dma = pltpu.SemaphoreType.DMA
    lower = jnp.transpose(lower, (1, 0, 2))
    upper = jnp.transpose(upper, (1, 0, 2))
    diag, llow, lup = diag[None], llow[None], lup[None]
    cols = NB * U
    lcols, ucols, rhs = (pltpu.with_memory_space_constraint(v, pltpu.HBM) for v in (lcols, ucols, rhs))
    lower, upper, diag, llow, lup = (pltpu.with_memory_space_constraint(v, pltpu.HBM) for v in (lower, upper, diag, llow, lup))
    scratch = [
        pltpu.VMEM((2, 32, 8, U * U), BF16),
        pltpu.VMEM((144 * PITCH, 128), F32),
        pltpu.VMEM((N2, cols), F32),
        pltpu.VMEM((N2, cols), F32),
        pltpu.VMEM((U, cols), F32),
        pltpu.VMEM((U, cols), F32),
        pltpu.VMEM((cols, 128), F32),
        dma((5, 2 * CHUNKS)),
        pltpu.VMEM((R, cols), F32),
        pltpu.VMEM((NB, KL), jnp.int32),
        pltpu.VMEM((NB, KL), jnp.int32),
        dma((3,)),
    ]
    if levels is None:
        outs = (jax.ShapeDtypeStruct((PACKED, 128), F32), jax.ShapeDtypeStruct((N2, cols), F32))
        params = pltpu.CompilerParams(vmem_limit_bytes=48000000)
    else:
        nx, nz, ny = levels
        outs = jax.ShapeDtypeStruct((R, cols), F32)
        scratch += [pltpu.VMEM((2, PACKED, 128), F32)]
        scratch += [pltpu.VMEM((n, 2 * HALF, 128), F32) for n in (ny, nz, nx)]
        scratch += [pltpu.VMEM((n, N2, 128), F32) for n in (ny // 2, nz // 2, nz // 4, 2)]
        scratch += [dma, dma] + [dma((n - 1,)) for n in (ny, nz, nx) for _ in range(4)]
        params = pltpu.CompilerParams(
            collective_id=0, has_side_effects=True, vmem_limit_bytes=48000000
        )
    return pl.pallas_call(
        functools.partial(kernel, levels),
        out_shape=outs,
        in_specs=[anywhere] * 8 + [pl.BlockSpec(memory_space=pltpu.SMEM)],
        out_specs=jax.tree.map(lambda _: vmem, outs),
        scratch_shapes=scratch,
        compiler_params=params,
        interpret=interpret,
        name="ilu_apply",
    )(rhs, lower, upper, diag, llow, lup, lcols, ucols, counts)


def solution(mesh, levels=LEVELS):
    both = ("chain", "side")
    return jax.shard_map(
        functools.partial(local, levels, False),
        mesh=mesh,
        in_specs=(
            P(None, both),
            P(both, None, None),
            P(both, None),
            P(both, None, None),
            P(both, None),
            P(both, None),
            P(both, None),
            P(both, None),
            P(both),
        ),
        out_specs=P(None, both),
        check_vma=False,
    )
```

```python
import functools

import jax
import jax.numpy as jnp
from jax import lax
from jax.experimental import pallas as pl
from jax.experimental.pallas import tpu as pltpu
from jax.sharding import PartitionSpec as P

U = 64
R = 8
NB = 16
KL = 13
N1 = R + U
N2 = R + 2 * U
PACKED = R + U + U // 2
PITCH = 72
HALF = 56
F32 = jnp.float32
BF16 = jnp.bfloat16
MESH = pl.DeviceIdType.MESH
NT = (((1,), (1,)), ((), ()))
NN = (((1,), (0,)), ((), ()))
LEVELS = (4, 8, 4)
CHUNKS = 2
PIECE = 4
GROUPS = 2 * KL + 3


def split(x):
    hi = x.astype(BF16)
    return hi, (x - hi.astype(F32)).astype(BF16)


def mm(a, b, dims):
    return lax.dot_general(a, b, dims, preferred_element_type=F32)


def dot3(x, w, dims=NN):
    m = x.shape[0]
    xh, xl = split(x)
    wh, wl = split(w)
    if dims == NT and w.shape[1] <= 128:
        both = jnp.concatenate(
            [jnp.concatenate([xh, xh], axis=1), jnp.concatenate([xl, xl], axis=1)], axis=0
        )
        both = mm(both, jnp.concatenate([wh, wl], axis=1), dims)
        return both[:m] + both[m:]
    both = jnp.concatenate([xh, xl], axis=0)
    if dims == NN and w.shape[1] % 128 == 0:
        n = w.shape[1]
        both = mm(both, jnp.concatenate([wh, wl], axis=1), dims)
        return both[:m, :n] + both[m:, :n] + both[:m, n:]
    both = mm(both, wh, dims)
    return both[:m] + both[m:] + mm(xh, wl, dims)


def dot2(x, w, dims=NN):
    m = x.shape[0]
    xh, xl = split(x)
    both = mm(jnp.concatenate([xh, xl], axis=0), w, dims)
    return both[:m] + both[m:]


def iota(shape, axis):
    return lax.broadcasted_iota(jnp.int32, shape, axis)


def lower_half():
    return iota((1, 128), 1) < U


def swap_halves(x):
    return pltpu.roll(x, U, axis=1)


def one_hot(lcols, ucols, active, half):
    e = iota((KL, 256), 0)
    group = iota((KL, 256), 1) // 8
    low = lcols[...].astype(F32).astype(BF16)
    up = ucols[...].astype(F32).astype(BF16)
    listed = mm(low, (group == e).astype(BF16), NN) + mm(up, (group == e + KL).astype(BF16), NN)
    lane = iota((1, 256), 1)
    group = lane // 8
    k = lane % 8 + 8 * half
    own = iota((NB, 256), 0) == iota((NB, 256), 1) % 8 + 8 * half
    target = jnp.sum(jnp.where(own, listed, 0.0), axis=0, keepdims=True).astype(jnp.int32)
    target = jnp.where(group == 2 * KL, k, target)
    target = jnp.where(group == 2 * KL + 1, 16, target)
    target = jnp.where(group == 2 * KL + 2, 17, target)
    target = jnp.where((group < GROUPS) & ((group == 2 * KL) | (k < active)), target, -1)
    r = iota((144, 256), 0)
    second = (r >= 72).astype(jnp.int32)
    column = 2 * (r // 8) - 17 * second
    return jnp.where((column == target) & (lane % 8 == r % 8), 1.0, 0.0).astype(BF16)


def assemble(sources, few, lcols, ucols, active, stack, panel, sems, hots, raw, fence):
    width = U * U // CHUNKS
    copies = {}
    for copy in few:
        copy.start()
    for half in range(2):
        for q in range(CHUNKS):
            lanes = pl.ds(width * q, width)
            row, first = [], 0
            for n, src in enumerate(sources):
                count = src.shape[0]
                copy = pltpu.make_async_copy(
                    src.at[:, pl.ds(8 * half, 8), lanes],
                    stack.at[half, pl.ds(first, count), :, lanes],
                    sems.at[n, half * CHUNKS + q],
                )
                copy.start()
                row.append(copy)
                first += count
            copies[half, q] = row
    stack[:, GROUPS:] = jnp.zeros((2, 32 - GROUPS, 8, U * U), BF16)
    low = lower_half()
    tiles = 16 // CHUNKS
    for copy in few:
        copy.wait()

    for half in range(2):
        hots[half] = one_hot(lcols, ucols, active, half)
    pieces = [(half, first) for half in range(2) for first in range(0, 16, PIECE)]
    for n in range(len(pieces) + 1):
        if n < len(pieces) and pieces[n][1] % tiles == 0:
            for copy in copies[pieces[n][0], pieces[n][1] // tiles]:
                copy.wait()

        @fence
        def _():
            if n < len(pieces):
                half, first = pieces[n]
                for t in range(PIECE):
                    lanes = pl.ds(256 * (first + t), 256)
                    raw[n % 2, t] = mm(hots[half], stack[half, :, :, lanes].reshape(256, 256), NN)
            if n:
                half, first = pieces[n - 1]
                for t in range(PIECE):
                    for s in range(2):
                        even = raw[(n - 1) % 2, t, 0:72, pl.ds(128 * s, 128)]
                        odd = raw[(n - 1) % 2, t, 72:144, pl.ds(128 * s, 128)]
                        i = 4 * (first + t) + 2 * s
                        panel[half][pl.ds(i, 72, stride=PITCH), :] = jnp.where(low, even, swap_halves(odd))
                        panel[half][pl.ds(i + 1, 72, stride=PITCH), :] = jnp.where(low, swap_halves(even), odd)


def block(panel, c2, k):
    return panel[k // 8][pl.ds((c2 * 8 + k % 8) * PITCH, U), :]


def column_blocks(panel, c2, first, last):
    return jnp.concatenate([block(panel, c2, k) for k in range(first, last)], axis=0)


def group_blocks(panel, s, first, last):
    return jnp.concatenate([column_blocks(panel, 2 * s + d, first, last) for d in range(2)], axis=1)


def operators(panel, ops, fops):
    low = lower_half()
    zeros = jnp.zeros((128, 128), F32)
    eye = jnp.where(iota((128, 128), 0) == iota((128, 128), 1), 1.0, 0.0)
    evens = [block(panel, c, 2 * c) for c in range(8)]
    odds = [block(panel, c, 2 * c + 1) for c in range(8)]
    fs = [eye - jnp.concatenate([zeros[:U], jnp.where(low, odd, 0.0)], axis=0) for odd in odds]
    lowers = [dot3(fs[2 * s + 1], column_blocks(panel, 2 * s, 4 * s + 2, 4 * s + 4)) for s in range(4)]
    inners = [dot3(even[:, :U], jnp.where(low, 0.0, even)) for even in evens]
    rights = [jnp.where(low, 0.0, odd) for odd in odds]
    inners = [swap_halves(inner)[:, :U] for inner in inners]
    inners = [dot2(inner, right.astype(BF16)) for inner, right in zip(inners, rights)]
    lowers = [dot3(lowers[s], fs[2 * s]) for s in range(4)]
    bs = [
        jnp.concatenate([jnp.where(low, even, -inner), right], axis=0)
        for even, inner, right in zip(evens, inners, rights)
    ]
    uppers = [dot3(bs[2 * s], column_blocks(panel, 2 * s + 1, 4 * s, 4 * s + 2)) for s in range(4)]
    for s in range(4):
        fops[s, 0:128, 0:128] = fs[2 * s]
        fops[s, 0:128, 128:256] = zeros
        fops[s, 128:256, 0:128] = -lowers[s]
        fops[s, 128:256, 128:256] = fs[2 * s + 1]
    uppers = [dot3(uppers[s], bs[2 * s + 1]) for s in range(4)]
    for s in range(4):
        ops[s, 0:128, 0:128] = bs[2 * s]
        ops[s, 0:128, 128:256] = -uppers[s]
        ops[s, 128:256, 0:128] = zeros
        ops[s, 128:256, 128:256] = bs[2 * s + 1]


def forward(rhs, active, panel, work, gt, hacc, ops, fops):
    low = lower_half()
    eye = (iota((128, 128), 0) == iota((128, 128), 1)).astype(BF16)
    last = jnp.zeros((N1, 128), F32)
    hacc[...] = jnp.where(iota((U, NB * U), 0) == iota((U, NB * U), 1), 1.0, 0.0)
    live = (iota((1, NB * U), 1) // U) < active
    work[0:R, :] = jnp.where(live, rhs[...], 0.0)
    work[R:, :] = -mm(eye, column_blocks(panel, 8, 0, NB).astype(BF16), NT)
    operators(panel, ops, fops)
    for s in range(4):
        here = pl.ds(256 * s, 256)
        x = dot3(work[0:N1, here], fops[s], NT)
        g = dot3(hacc[:, here], ops[s])
        if s < 3:
            rest = pl.ds(256 * (s + 1), 256 * (3 - s))
            work[0:N1, rest] -= dot3(x, group_blocks(panel, s, 4 * s + 4, NB), NT)
            weights = [group_blocks(panel, d, 4 * s, 4 * s + 4) for d in range(s + 1, 4)]
            hacc[:, rest] -= dot3(g, jnp.concatenate(weights, axis=1))
        work[0:N1, here] = x
        gt[:, here] = g
        for d in range(2):
            mine = 4 * s + 2 * d + jnp.where(low, 0, 1) == active - 1
            last = last + jnp.where(mine, x[:, 128 * d : 128 * d + 128], 0.0)
    boundary = last + swap_halves(last)
    weights = jnp.concatenate([jnp.zeros((U, NB * U), F32), gt[...]], axis=0)
    z0 = dot3(work[...], weights, NT)
    return jnp.concatenate([jnp.where(low, boundary, z0[:N1]), z0[N1:]], axis=0)


def backward_step(s, panel, work, zbuf, ops):
    here = pl.ds(256 * s, 256)
    z = dot3(work[:, here], ops[s], NT)
    zbuf[:, here] = z
    if s:
        work[:, pl.ds(0, 256 * s)] -= dot3(z, group_blocks(panel, s, 0, 4 * s), NT)


def unpack(m):
    low = lower_half()
    d = m[N1:]
    return jnp.concatenate(
        [m[:N1], jnp.where(low, 0.0, swap_halves(d)), jnp.where(low, 0.0, d)], axis=0
    )


def pack(m):
    top, bottom = m[N1 : N1 + U // 2], m[N1 + U // 2 :]
    return jnp.concatenate([m[:N1], jnp.where(lower_half(), swap_halves(top), bottom)], axis=0)


def compose(left, right):
    t = dot3(left[:N1, :U], right[R:N1])
    t = jnp.concatenate([t[:R] + right[:R], t[R:]], axis=0)
    weights = jnp.concatenate([jnp.zeros((U, 128), F32), left[N1:]], axis=0)
    s = dot3(jnp.concatenate([t, right[N1:]], axis=0), weights)
    return jnp.concatenate([jnp.where(lower_half(), t, s[:N1] + left[:N1]), s[N1:]], axis=0)


def identity_map():
    r = iota((N2, 128), 0)
    lane = iota((N2, 128), 1)
    one = ((r >= R) & (r < N1) & (lane == r - R)) | ((r >= N1) & (lane == r - N1 + U))
    return jnp.where(one, 1.0, 0.0)


def narrow(right, sibling, before, after):
    c = compose(jnp.where(right, sibling, after), jnp.where(right, before, sibling))
    return jnp.where(right, c, before), jnp.where(right, after, c)


def kernel(
    levels, rhs_in, lower, upper, diag, llow, lup, lcols_in, ucols_in, counts, *rest
):
    if levels is None:
        maps, zout, stack, panel0, panel1, work, zbuf, gt, hacc, ops, fops, in_sems, rhs, lcols, ucols, few_sems, hots, raw = rest
        few = [
            pltpu.make_async_copy(src, dst, few_sems.at[n])
            for n, (src, dst) in enumerate(((lcols_in, lcols), (ucols_in, ucols), (rhs_in, rhs)))
        ]
        active = counts[0]
        panel = (panel0, panel1)
        fence = lambda f: f()
        assemble((lower, upper, diag, llow, lup), few, lcols, ucols, active, stack, panel, in_sems, hots, raw, fence)
        maps[...] = pack(forward(rhs, active, panel, work, gt, hacc, ops, fops))
        for s in reversed(range(4)):
            backward_step(s, panel, work, zout, ops)
        return
    (
        out, stack, panel0, panel1, work, zbuf, gt, hacc, ops, fops, in_sems, rhs, lcols, ucols, few_sems, hots, raw,
        b_core, b_y, b_z, b_x, y_pairs, z_pairs, z_quads, sides,
        s_core, r_core, s_y, r_y, s_fy, r_fy, s_z, r_z, s_fz, r_fz, s_x, r_x, s_fx, r_fx,
    ) = rest
    nx, nz, ny = levels
    chain = lax.axis_index("chain")
    side = lax.axis_index("side")
    y = chain % ny
    zz = (chain // ny) % nz
    x = chain // (ny * nz)

    def at_core():
        return (chain, 1 - side)

    def at_y(k):
        return (chain - y + (y + k) % ny, side)

    def at_z(k):
        return (chain - zz * ny + ((zz + k) % nz) * ny, side)

    def at_x(k):
        return (((x + k) % nx) * (ny * nz) + chain % (ny * nz), side)

    peers = [at_core()]
    peers += [at_y(k) for k in range(1, ny)]
    peers += [at_z(k) for k in range(1, nz)]
    peers += [at_x(k) for k in range(1, nx)]
    barrier = pltpu.get_barrier_semaphore()
    for peer in peers:
        pl.semaphore_signal(barrier, inc=1, device_id=peer, device_id_type=MESH)

    def remote(src, dst, send, recv, peer):
        return pltpu.make_async_remote_copy(
            src_ref=src, dst_ref=dst, send_sem=send, recv_sem=recv, device_id=peer, device_id_type=MESH
        )

    mine = pl.ds(pl.multiple_of(side * HALF, 8), HALF)

    def put(buf, index, m):
        buf[index, 0:PACKED] = pack(m)
        buf[index, PACKED:] = jnp.zeros((2 * HALF - PACKED, 128), F32)

    def ring(buf, index, count, peer_of, send, recv, send_on, recv_on):
        arrivals, handovers = [], []
        for k in sorted(range(1, count), key=lambda k: min(k, count - k)):
            part = buf.at[index, mine]
            arrivals.append(remote(part, part, send.at[k - 1], recv.at[k - 1], peer_of(k)))
            part = buf.at[(index + count - k) % count, mine]
            handovers.append(remote(part, part, send_on.at[k - 1], recv_on.at[k - 1], at_core()))
        for copy in arrivals:
            copy.start()
        return arrivals, handovers

    def finish(copies):
        for arriving, handover in zip(*copies):
            arriving.wait_recv()
            handover.start()
        for arriving in copies[0]:
            arriving.wait_send()
        for handover in copies[1]:
            handover.wait()

    few = [
        pltpu.make_async_copy(src, dst, few_sems.at[n])
        for n, (src, dst) in enumerate(((lcols_in, lcols), (ucols_in, ucols), (rhs_in, rhs)))
    ]
    active = counts[0]
    panel = (panel0, panel1)
    fence = pl.when(chain + zz < 777)
    assemble((lower, upper, diag, llow, lup), few, lcols, ucols, active, stack, panel, in_sems, hots, raw, fence)
    b_core[side] = pack(forward(rhs, active, panel, work, gt, hacc, ops, fops))
    pl.semaphore_wait(barrier, len(peers))

    core = remote(b_core.at[side], b_core.at[side], s_core, r_core, at_core())
    core.start()
    core.wait()

    @fence
    def _():
        put(b_y, y, compose(unpack(b_core[0]), unpack(b_core[1])))

    ys = ring(b_y, y, ny, at_y, s_y, r_y, s_fy, r_fy)

    @fence
    def _():
        for s in (3, 2):
            backward_step(s, panel, work, zbuf, ops)

    finish(ys)

    @fence
    def _():
        nodes = [compose(unpack(b_y[i, 0:PACKED]), unpack(b_y[i + 1, 0:PACKED])) for i in range(0, ny, 2)]
        for i, node in enumerate(nodes):
            y_pairs[i] = node
        put(b_z, zz, compose(*nodes))

    zs = ring(b_z, zz, nz, at_z, s_z, r_z, s_fz, r_fz)

    @fence
    def _():
        for s in (1, 0):
            backward_step(s, panel, work, zbuf, ops)

    @fence
    def _():
        before = after = identity_map()
        before, after = narrow(side == 1, unpack(b_core[1 - side]), before, after)
        before, after = narrow(y % 2 == 1, unpack(b_y[y + 1 - 2 * (y % 2), 0:PACKED]), before, after)
        before, after = narrow(y // 2 == 1, y_pairs[1 - y // 2], before, after)
        sides[0] = before
        sides[1] = after

    finish(zs)

    @fence
    def _():
        nodes = [compose(unpack(b_z[i, 0:PACKED]), unpack(b_z[i + 1, 0:PACKED])) for i in range(0, nz, 2)]
        for i, node in enumerate(nodes):
            z_pairs[i] = node
        nodes = [compose(nodes[i], nodes[i + 1]) for i in range(0, nz // 2, 2)]
        for i, node in enumerate(nodes):
            z_quads[i] = node
        put(b_x, x, compose(*nodes))

    xs = ring(b_x, x, nx, at_x, s_x, r_x, s_fx, r_fx)

    @fence
    def _():
        before, after = sides[0], sides[1]
        before, after = narrow(zz % 2 == 1, unpack(b_z[zz + 1 - 2 * (zz % 2), 0:PACKED]), before, after)
        pair = zz // 2
        before, after = narrow(pair % 2 == 1, z_pairs[pair + 1 - 2 * (pair % 2)], before, after)
        before, after = narrow(zz // 4 == 1, z_quads[1 - zz // 4], before, after)
        sides[0] = before
        sides[1] = after

    finish(xs)

    t = b_x[0, 0:R]
    p = jnp.zeros((R, U), F32)
    ends = [t]
    for j in range(1, nx):
        p = jnp.where(x == j, t[:, :U], p)
        t = dot3(t[:, :U], b_x[j, R:N1]) + b_x[j, 0:R]
        ends.append(t)
    q_run = ends[nx - 1][:, U:]
    q = jnp.zeros((R, U), F32)
    for j in reversed(range(nx - 1)):
        q = jnp.where(x == j, q_run, q)
        if j:
            q_run = dot3(q_run, unpack(b_x[j, 0:PACKED])[N1:, U:]) + ends[j][:, U:]
    own = unpack(b_core[side])
    before, after = sides[0], sides[1]
    p = dot3(p, before[R:N1, :U]) + before[:R, :U]
    t = dot3(p, own[R:N1, :U]) + own[:R, :U]
    t = dot3(t, after[R:N1]) + after[:R]
    q = t[:, U:] + dot3(q, after[N1:, U:])
    out[...] = zbuf[0:R, :] + dot3(jnp.concatenate([p, q], axis=1), zbuf[R:, :])


def local(levels, interpret, rhs, lower, lcols, upper, ucols, diag, llow, lup, counts):
    vmem = pl.BlockSpec(memory_space=pltpu.VMEM)
    anywhere = pl.BlockSpec(memory_space=pl.ANY)
    dma = pltpu.SemaphoreType.DMA
    lower = jnp.transpose(lower, (1, 0, 2))
    upper = jnp.transpose(upper, (1, 0, 2))
    diag, llow, lup = diag[None], llow[None], lup[None]
    cols = NB * U
    lcols, ucols, rhs = (pltpu.with_memory_space_constraint(v, pltpu.HBM) for v in (lcols, ucols, rhs))
    lower, upper, diag, llow, lup = (pltpu.with_memory_space_constraint(v, pltpu.HBM) for v in (lower, upper, diag, llow, lup))
    scratch = [
        pltpu.VMEM((2, 32, 8, U * U), BF16),
        pltpu.VMEM((72 * PITCH, 128), F32),
        pltpu.VMEM((72 * PITCH, 128), F32),
        pltpu.VMEM((N2, cols), F32),
        pltpu.VMEM((N2, cols), F32),
        pltpu.VMEM((U, cols), F32),
        pltpu.VMEM((U, cols), F32),
        pltpu.VMEM((4, 256, 256), F32),
        pltpu.VMEM((4, 256, 256), F32),
        dma((5, 2 * CHUNKS)),
        pltpu.VMEM((R, cols), F32),
        pltpu.VMEM((NB, KL), jnp.int32),
        pltpu.VMEM((NB, KL), jnp.int32),
        dma((3,)),
        pltpu.VMEM((2, 144, 256), BF16),
        pltpu.VMEM((2, PIECE, 144, 256), F32),
    ]
    if levels is None:
        outs = (jax.ShapeDtypeStruct((PACKED, 128), F32), jax.ShapeDtypeStruct((N2, cols), F32))
        params = pltpu.CompilerParams(vmem_limit_bytes=48000000)
    else:
        nx, nz, ny = levels
        outs = jax.ShapeDtypeStruct((R, cols), F32)
        scratch += [pltpu.VMEM((2, PACKED, 128), F32)]
        scratch += [pltpu.VMEM((n, 2 * HALF, 128), F32) for n in (ny, nz, nx)]
        scratch += [pltpu.VMEM((n, N2, 128), F32) for n in (ny // 2, nz // 2, nz // 4, 2)]
        scratch += [dma, dma] + [dma((n - 1,)) for n in (ny, nz, nx) for _ in range(4)]
        params = pltpu.CompilerParams(
            collective_id=0, has_side_effects=True, vmem_limit_bytes=48000000
        )
    return pl.pallas_call(
        functools.partial(kernel, levels),
        out_shape=outs,
        in_specs=[anywhere] * 8 + [pl.BlockSpec(memory_space=pltpu.SMEM)],
        out_specs=jax.tree.map(lambda _: vmem, outs),
        scratch_shapes=scratch,
        compiler_params=params,
        interpret=interpret,
        name="ilu_apply",
    )(rhs, lower, upper, diag, llow, lup, lcols, ucols, counts)


def solution(mesh, levels=LEVELS):
    both = ("chain", "side")
    return jax.shard_map(
        functools.partial(local, levels, False),
        mesh=mesh,
        in_specs=(
            P(None, both),
            P(both, None, None),
            P(both, None),
            P(both, None, None),
            P(both, None),
            P(both, None),
            P(both, None),
            P(both, None),
            P(both),
        ),
        out_specs=P(None, both),
        check_vma=False,
    )
```

```python
import functools

import jax
import jax.numpy as jnp
from jax import lax
from jax.experimental import pallas as pl
from jax.experimental.pallas import tpu as pltpu
from jax.sharding import PartitionSpec as P

U = 64
R = 8
NB = 16
KL = 13
N1 = R + U
N2 = R + 2 * U
PACKED = R + U + U // 2
PITCH = 72
F32 = jnp.float32
BF16 = jnp.bfloat16
MESH = pl.DeviceIdType.MESH
NT = (((1,), (1,)), ((), ()))
NN = (((1,), (0,)), ((), ()))
LEVELS = (4, 8, 4)
CHUNKS = 2
PIECE = 4
GROUPS = 2 * KL + 3


def split(x):
    hi = x.astype(BF16)
    return hi, (x - hi.astype(F32)).astype(BF16)


def mm(a, b, dims):
    return lax.dot_general(a, b, dims, preferred_element_type=F32)


def dot3(x, w, dims=NN):
    m = x.shape[0]
    xh, xl = split(x)
    wh, wl = split(w)
    if dims == NT and w.shape[1] <= 128:
        both = jnp.concatenate(
            [jnp.concatenate([xh, xh], axis=1), jnp.concatenate([xl, xl], axis=1)], axis=0
        )
        both = mm(both, jnp.concatenate([wh, wl], axis=1), dims)
        return both[:m] + both[m:]
    both = jnp.concatenate([xh, xl], axis=0)
    if dims == NN and w.shape[1] % 128 == 0:
        n = w.shape[1]
        both = mm(both, jnp.concatenate([wh, wl], axis=1), dims)
        return both[:m, :n] + both[m:, :n] + both[:m, n:]
    both = mm(both, wh, dims)
    return both[:m] + both[m:] + mm(xh, wl, dims)


def dot2(x, w, dims=NN):
    m = x.shape[0]
    xh, xl = split(x)
    both = mm(jnp.concatenate([xh, xl], axis=0), w, dims)
    return both[:m] + both[m:]


def iota(shape, axis):
    return lax.broadcasted_iota(jnp.int32, shape, axis)


def lower_half():
    return iota((1, 128), 1) < U


def swap_halves(x):
    return pltpu.roll(x, U, axis=1)


def one_hot(lcols, ucols, active, half):
    e = iota((KL, 256), 0)
    group = iota((KL, 256), 1) // 8
    low = lcols[...].astype(F32).astype(BF16)
    up = ucols[...].astype(F32).astype(BF16)
    listed = mm(low, (group == e).astype(BF16), NN) + mm(up, (group == e + KL).astype(BF16), NN)
    lane = iota((1, 256), 1)
    group = lane // 8
    k = lane % 8 + 8 * half
    own = iota((NB, 256), 0) == iota((NB, 256), 1) % 8 + 8 * half
    target = jnp.sum(jnp.where(own, listed, 0.0), axis=0, keepdims=True).astype(jnp.int32)
    target = jnp.where(group == 2 * KL, k, target)
    target = jnp.where(group == 2 * KL + 1, 16, target)
    target = jnp.where(group == 2 * KL + 2, 17, target)
    target = jnp.where((group < GROUPS) & ((group == 2 * KL) | (k < active)), target, -1)
    r = iota((144, 256), 0)
    second = (r >= 72).astype(jnp.int32)
    column = 2 * (r // 8) - 17 * second
    return jnp.where((column == target) & (lane % 8 == r % 8), 1.0, 0.0).astype(BF16)


def assemble(sources, few, lcols, ucols, active, stack, panel, sems, hots, raw, fence):
    width = U * U // CHUNKS
    copies = {}
    for copy in few:
        copy.start()
    for half in range(2):
        for q in range(CHUNKS):
            lanes = pl.ds(width * q, width)
            row, first = [], 0
            for n, src in enumerate(sources):
                count = src.shape[0]
                copy = pltpu.make_async_copy(
                    src.at[:, pl.ds(8 * half, 8), lanes],
                    stack.at[half, pl.ds(first, count), :, lanes],
                    sems.at[n, half * CHUNKS + q],
                )
                copy.start()
                row.append(copy)
                first += count
            copies[half, q] = row
    stack[:, GROUPS:] = jnp.zeros((2, 32 - GROUPS, 8, U * U), BF16)
    low = lower_half()
    tiles = 16 // CHUNKS
    for copy in few:
        copy.wait()

    for half in range(2):
        hots[half] = one_hot(lcols, ucols, active, half)
    pieces = [(half, first) for half in range(2) for first in range(0, 16, PIECE)]
    for n in range(len(pieces) + 1):
        if n < len(pieces) and pieces[n][1] % tiles == 0:
            for copy in copies[pieces[n][0], pieces[n][1] // tiles]:
                copy.wait()

        @fence
        def _():
            if n < len(pieces):
                half, first = pieces[n]
                for t in range(PIECE):
                    lanes = pl.ds(256 * (first + t), 256)
                    raw[n % 2, t] = mm(hots[half], stack[half, :, :, lanes].reshape(256, 256), NN)
            if n:
                half, first = pieces[n - 1]
                for t in range(PIECE):
                    for s in range(2):
                        even = raw[(n - 1) % 2, t, 0:72, pl.ds(128 * s, 128)]
                        odd = raw[(n - 1) % 2, t, 72:144, pl.ds(128 * s, 128)]
                        i = 4 * (first + t) + 2 * s
                        panel[half][pl.ds(i, 72, stride=PITCH), :] = jnp.where(low, even, swap_halves(odd))
                        panel[half][pl.ds(i + 1, 72, stride=PITCH), :] = jnp.where(low, swap_halves(even), odd)


def block(panel, c2, k):
    return panel[k // 8][pl.ds((c2 * 8 + k % 8) * PITCH, U), :]


def column_blocks(panel, c2, first, last):
    return jnp.concatenate([block(panel, c2, k) for k in range(first, last)], axis=0)


def group_blocks(panel, s, first, last):
    return jnp.concatenate([column_blocks(panel, 2 * s + d, first, last) for d in range(2)], axis=1)


def operators(panel, ops, fops):
    low = lower_half()
    zeros = jnp.zeros((128, 128), F32)
    eye = jnp.where(iota((128, 128), 0) == iota((128, 128), 1), 1.0, 0.0)
    evens = [block(panel, c, 2 * c) for c in range(8)]
    odds = [block(panel, c, 2 * c + 1) for c in range(8)]
    fs = [eye - jnp.concatenate([zeros[:U], jnp.where(low, odd, 0.0)], axis=0) for odd in odds]
    lowers = [dot3(fs[2 * s + 1], column_blocks(panel, 2 * s, 4 * s + 2, 4 * s + 4)) for s in range(4)]
    inners = [dot3(even[:, :U], jnp.where(low, 0.0, even)) for even in evens]
    rights = [jnp.where(low, 0.0, odd) for odd in odds]
    inners = [swap_halves(inner)[:, :U] for inner in inners]
    inners = [dot2(inner, right.astype(BF16)) for inner, right in zip(inners, rights)]
    lowers = [dot3(lowers[s], fs[2 * s]) for s in range(4)]
    bs = [
        jnp.concatenate([jnp.where(low, even, -inner), right], axis=0)
        for even, inner, right in zip(evens, inners, rights)
    ]
    uppers = [dot3(bs[2 * s], column_blocks(panel, 2 * s + 1, 4 * s, 4 * s + 2)) for s in range(4)]
    for s in range(4):
        fops[s, 0:128, 0:128] = fs[2 * s]
        fops[s, 0:128, 128:256] = zeros
        fops[s, 128:256, 0:128] = -lowers[s]
        fops[s, 128:256, 128:256] = fs[2 * s + 1]
    uppers = [dot3(uppers[s], bs[2 * s + 1]) for s in range(4)]
    for s in range(4):
        ops[s, 0:128, 0:128] = bs[2 * s]
        ops[s, 0:128, 128:256] = -uppers[s]
        ops[s, 128:256, 0:128] = zeros
        ops[s, 128:256, 128:256] = bs[2 * s + 1]


def forward(rhs, active, panel, work, gt, hacc, ops, fops):
    low = lower_half()
    eye = (iota((128, 128), 0) == iota((128, 128), 1)).astype(BF16)
    last = jnp.zeros((N1, 128), F32)
    hacc[...] = jnp.where(iota((U, NB * U), 0) == iota((U, NB * U), 1), 1.0, 0.0)
    live = (iota((1, NB * U), 1) // U) < active
    work[0:R, :] = jnp.where(live, rhs[...], 0.0)
    work[R:, :] = -mm(eye, column_blocks(panel, 8, 0, NB).astype(BF16), NT)
    operators(panel, ops, fops)
    for s in range(4):
        here = pl.ds(256 * s, 256)
        x = dot3(work[0:N1, here], fops[s], NT)
        g = dot3(hacc[:, here], ops[s])
        if s < 3:
            rest = pl.ds(256 * (s + 1), 256 * (3 - s))
            work[0:N1, rest] -= dot3(x, group_blocks(panel, s, 4 * s + 4, NB), NT)
            weights = [group_blocks(panel, d, 4 * s, 4 * s + 4) for d in range(s + 1, 4)]
            hacc[:, rest] -= dot3(g, jnp.concatenate(weights, axis=1))
        work[0:N1, here] = x
        gt[:, here] = g
        for d in range(2):
            mine = 4 * s + 2 * d + jnp.where(low, 0, 1) == active - 1
            last = last + jnp.where(mine, x[:, 128 * d : 128 * d + 128], 0.0)
    boundary = last + swap_halves(last)
    weights = jnp.concatenate([jnp.zeros((U, NB * U), F32), gt[...]], axis=0)
    z0 = dot3(work[...], weights, NT)
    return jnp.concatenate([jnp.where(low, boundary, z0[:N1]), z0[N1:]], axis=0)


def backward_step(s, panel, work, zbuf, ops):
    here = pl.ds(256 * s, 256)
    z = dot3(work[:, here], ops[s], NT)
    zbuf[:, here] = z
    if s:
        work[:, pl.ds(0, 256 * s)] -= dot3(z, group_blocks(panel, s, 0, 4 * s), NT)


def unpack(m):
    low = lower_half()
    d = m[N1:]
    return jnp.concatenate(
        [m[:N1], jnp.where(low, 0.0, swap_halves(d)), jnp.where(low, 0.0, d)], axis=0
    )


def pack(m):
    top, bottom = m[N1 : N1 + U // 2], m[N1 + U // 2 :]
    return jnp.concatenate([m[:N1], jnp.where(lower_half(), swap_halves(top), bottom)], axis=0)


def compose(left, right):
    t = dot3(left[:N1, :U], right[R:N1])
    t = jnp.concatenate([t[:R] + right[:R], t[R:]], axis=0)
    weights = jnp.concatenate([jnp.zeros((U, 128), F32), left[N1:]], axis=0)
    s = dot3(jnp.concatenate([t, right[N1:]], axis=0), weights)
    return jnp.concatenate([jnp.where(lower_half(), t, s[:N1] + left[:N1]), s[N1:]], axis=0)


def identity_map():
    r = iota((N2, 128), 0)
    lane = iota((N2, 128), 1)
    one = ((r >= R) & (r < N1) & (lane == r - R)) | ((r >= N1) & (lane == r - N1 + U))
    return jnp.where(one, 1.0, 0.0)


def narrow(right, sibling, before, after):
    c = compose(jnp.where(right, sibling, after), jnp.where(right, before, sibling))
    return jnp.where(right, c, before), jnp.where(right, after, c)


def kernel(
    levels, rhs_in, lower, upper, diag, llow, lup, lcols_in, ucols_in, counts, *rest
):
    if levels is None:
        maps, zout, stack, panel0, panel1, work, zbuf, gt, hacc, ops, fops, in_sems, rhs, lcols, ucols, few_sems, hots, raw = rest
        few = [
            pltpu.make_async_copy(src, dst, few_sems.at[n])
            for n, (src, dst) in enumerate(((lcols_in, lcols), (ucols_in, ucols), (rhs_in, rhs)))
        ]
        active = counts[0]
        panel = (panel0, panel1)
        fence = lambda f: f()
        assemble((lower, upper, diag, llow, lup), few, lcols, ucols, active, stack, panel, in_sems, hots, raw, fence)
        maps[...] = pack(forward(rhs, active, panel, work, gt, hacc, ops, fops))
        for s in reversed(range(4)):
            backward_step(s, panel, work, zout, ops)
        return
    (
        out, stack, panel0, panel1, work, zbuf, gt, hacc, ops, fops, in_sems, rhs, lcols, ucols, few_sems, hots, raw,
        b_core, b_y, b_z, b_x, b_half, y_pairs, z_pairs, z_near, sides,
        s_core, r_core, s_half, r_half, s_sib, r_sib, s_y, r_y, s_z, r_z, s_x, r_x,
    ) = rest
    nx, nz, ny = levels
    chain = lax.axis_index("chain")
    side = lax.axis_index("side")
    y = chain % ny
    zz = (chain // ny) % nz
    x = chain // (ny * nz)

    def at_core():
        return (chain, 1 - side)

    def at_y(k):
        return (chain - y + (y + k) % ny, side)

    def at_z(k, core):
        return (chain - zz * ny + ((zz + k) % nz) * ny, core)

    def at_x(k):
        return (((x + k) % nx) * (ny * nz) + chain % (ny * nz), side)

    peers = [at_core()]
    peers += [at_y(k) for k in range(1, ny)]
    peers += [at_z(k, core) for k in range(1, nz) for core in range(2)]
    peers += [at_x(k) for k in range(1, nx)]
    barrier = pltpu.get_barrier_semaphore()
    for peer in peers:
        pl.semaphore_signal(barrier, inc=1, device_id=peer, device_id_type=MESH)

    def remote(src, dst, send, recv, peer):
        return pltpu.make_async_remote_copy(
            src_ref=src, dst_ref=dst, send_sem=send, recv_sem=recv, device_id=peer, device_id_type=MESH
        )

    def ring(buf, index, count, peer_of, send, recv):
        copies = []
        for k in sorted(range(1, count), key=lambda k: min(k, count - k)):
            copies.append(remote(buf.at[index], buf.at[index], send.at[k - 1], recv.at[k - 1], peer_of(k)))
        for copy in copies:
            copy.start()
        return copies

    def finish(copies):
        for copy in copies:
            copy.wait()

    half = nz // 2
    home = zz // half
    order = sorted(range(1, nz), key=lambda k: min(k, nz - k))

    def z_copy(k):
        return remote(b_z.at[zz], b_z.at[zz], s_z.at[k - 1], r_z.at[k - 1], at_z(k, home))

    def z_start():
        for k in order:
            @pl.when(side == (0 if k <= half else 1))
            def _():
                z_copy(k).start()

    def z_finish():
        for k in order:
            @pl.when(((zz + nz - k) % nz) // half == side)
            def _():
                z_copy(k).wait_recv()
        for k in order:
            @pl.when(side == (0 if k <= half else 1))
            def _():
                z_copy(k).wait_send()

    few = [
        pltpu.make_async_copy(src, dst, few_sems.at[n])
        for n, (src, dst) in enumerate(((lcols_in, lcols), (ucols_in, ucols), (rhs_in, rhs)))
    ]
    active = counts[0]
    panel = (panel0, panel1)
    fence = pl.when(chain + zz < 777)
    assemble((lower, upper, diag, llow, lup), few, lcols, ucols, active, stack, panel, in_sems, hots, raw, fence)
    b_core[side] = pack(forward(rhs, active, panel, work, gt, hacc, ops, fops))
    pl.semaphore_wait(barrier, len(peers))

    core = remote(b_core.at[side], b_core.at[side], s_core, r_core, at_core())
    core.start()
    core.wait()

    @fence
    def _():
        b_y[y] = pack(compose(unpack(b_core[0]), unpack(b_core[1])))

    ys = ring(b_y, y, ny, at_y, s_y, r_y)

    @fence
    def _():
        for s in (3, 2):
            backward_step(s, panel, work, zbuf, ops)

    finish(ys)

    @fence
    def _():
        nodes = [compose(unpack(b_y[i]), unpack(b_y[i + 1])) for i in range(0, ny, 2)]
        for i, node in enumerate(nodes):
            y_pairs[i] = node
        b_z[zz] = pack(compose(*nodes))

    z_start()

    @fence
    def _():
        for s in (1, 0):
            backward_step(s, panel, work, zbuf, ops)

    @fence
    def _():
        before = after = identity_map()
        before, after = narrow(side == 1, unpack(b_core[1 - side]), before, after)
        before, after = narrow(y % 2 == 1, unpack(b_y[y + 1 - 2 * (y % 2)]), before, after)
        before, after = narrow(y // 2 == 1, y_pairs[1 - y // 2], before, after)
        sides[0] = before
        sides[1] = after

    z_finish()
    first = side * half
    sibling = zz + 1 - 2 * (zz % 2)

    @fence
    def _():
        nodes = [compose(unpack(b_z[first + i]), unpack(b_z[first + i + 1])) for i in range(0, half, 2)]
        for i, node in enumerate(nodes):
            z_pairs[i] = node
        b_half[side] = pack(compose(*nodes))

    swap = remote(b_half.at[side], b_half.at[side], s_half, r_half, at_core())
    swap.start()
    leaf = remote(b_z.at[sibling], b_z.at[sibling], s_sib.at[0], r_sib.at[0], at_core())
    near = remote(z_near, z_near, s_sib.at[1], r_sib.at[1], at_core())

    @pl.when(home == side)
    def _():
        z_near[...] = z_pairs[1 - (zz % half) // 2]
        leaf.start()
        near.start()

    swap.wait()

    @fence
    def _():
        b_x[x] = pack(compose(unpack(b_half[0]), unpack(b_half[1])))

    xs = ring(b_x, x, nx, at_x, s_x, r_x)

    @pl.when(home == side)
    def _():
        leaf.wait_send()
        near.wait_send()

    @pl.when(home != side)
    def _():
        leaf.wait_recv()
        near.wait_recv()

    @fence
    def _():
        before, after = sides[0], sides[1]
        before, after = narrow(zz % 2 == 1, unpack(b_z[sibling]), before, after)
        before, after = narrow((zz % half) // 2 == 1, z_near[...], before, after)
        before, after = narrow(home == 1, unpack(b_half[1 - home]), before, after)
        sides[0] = before
        sides[1] = after

    finish(xs)

    t = b_x[0, 0:R]
    p = jnp.zeros((R, U), F32)
    ends = [t]
    for j in range(1, nx):
        p = jnp.where(x == j, t[:, :U], p)
        t = dot3(t[:, :U], b_x[j, R:N1]) + b_x[j, 0:R]
        ends.append(t)
    q_run = ends[nx - 1][:, U:]
    q = jnp.zeros((R, U), F32)
    for j in reversed(range(nx - 1)):
        q = jnp.where(x == j, q_run, q)
        if j:
            q_run = dot3(q_run, unpack(b_x[j])[N1:, U:]) + ends[j][:, U:]
    own = unpack(b_core[side])
    before, after = sides[0], sides[1]
    p = dot3(p, before[R:N1, :U]) + before[:R, :U]
    t = dot3(p, own[R:N1, :U]) + own[:R, :U]
    t = dot3(t, after[R:N1]) + after[:R]
    q = t[:, U:] + dot3(q, after[N1:, U:])
    out[...] = zbuf[0:R, :] + dot3(jnp.concatenate([p, q], axis=1), zbuf[R:, :])


def local(levels, interpret, rhs, lower, lcols, upper, ucols, diag, llow, lup, counts):
    vmem = pl.BlockSpec(memory_space=pltpu.VMEM)
    anywhere = pl.BlockSpec(memory_space=pl.ANY)
    dma = pltpu.SemaphoreType.DMA
    lower = jnp.transpose(lower, (1, 0, 2))
    upper = jnp.transpose(upper, (1, 0, 2))
    diag, llow, lup = diag[None], llow[None], lup[None]
    cols = NB * U
    lcols, ucols, rhs = (pltpu.with_memory_space_constraint(v, pltpu.HBM) for v in (lcols, ucols, rhs))
    lower, upper, diag, llow, lup = (pltpu.with_memory_space_constraint(v, pltpu.HBM) for v in (lower, upper, diag, llow, lup))
    scratch = [
        pltpu.VMEM((2, 32, 8, U * U), BF16),
        pltpu.VMEM((72 * PITCH, 128), F32),
        pltpu.VMEM((72 * PITCH, 128), F32),
        pltpu.VMEM((N2, cols), F32),
        pltpu.VMEM((N2, cols), F32),
        pltpu.VMEM((U, cols), F32),
        pltpu.VMEM((U, cols), F32),
        pltpu.VMEM((4, 256, 256), F32),
        pltpu.VMEM((4, 256, 256), F32),
        dma((5, 2 * CHUNKS)),
        pltpu.VMEM((R, cols), F32),
        pltpu.VMEM((NB, KL), jnp.int32),
        pltpu.VMEM((NB, KL), jnp.int32),
        dma((3,)),
        pltpu.VMEM((2, 144, 256), BF16),
        pltpu.VMEM((2, PIECE, 144, 256), F32),
    ]
    if levels is None:
        outs = (jax.ShapeDtypeStruct((PACKED, 128), F32), jax.ShapeDtypeStruct((N2, cols), F32))
        params = pltpu.CompilerParams(vmem_limit_bytes=48000000)
    else:
        nx, nz, ny = levels
        outs = jax.ShapeDtypeStruct((R, cols), F32)
        scratch += [pltpu.VMEM((n, PACKED, 128), F32) for n in (2, ny, nz, nx, 2)]
        scratch += [pltpu.VMEM(m + (N2, 128), F32) for m in ((ny // 2,), (nz // 4,), (), (2,))]
        scratch += [dma] * 4 + [dma((2,))] * 2 + [dma((n - 1,)) for n in (ny, ny, nz, nz, nx, nx)]
        params = pltpu.CompilerParams(
            collective_id=0, has_side_effects=True, vmem_limit_bytes=48000000
        )
    return pl.pallas_call(
        functools.partial(kernel, levels),
        out_shape=outs,
        in_specs=[anywhere] * 8 + [pl.BlockSpec(memory_space=pltpu.SMEM)],
        out_specs=jax.tree.map(lambda _: vmem, outs),
        scratch_shapes=scratch,
        compiler_params=params,
        interpret=interpret,
        name="ilu_apply",
    )(rhs, lower, upper, diag, llow, lup, lcols, ucols, counts)


def solution(mesh, levels=LEVELS):
    both = ("chain", "side")
    return jax.shard_map(
        functools.partial(local, levels, False),
        mesh=mesh,
        in_specs=(
            P(None, both),
            P(both, None, None),
            P(both, None),
            P(both, None, None),
            P(both, None),
            P(both, None),
            P(both, None),
            P(both, None),
            P(both),
        ),
        out_specs=P(None, both),
        check_vma=False,
    )
```

```python
import functools

import jax
import jax.numpy as jnp
from jax import lax
from jax.experimental import pallas as pl
from jax.experimental.pallas import tpu as pltpu
from jax.sharding import PartitionSpec as P

U = 64
R = 8
NB = 16
KL = 13
N1 = R + U
N2 = R + 2 * U
PACKED = R + U + U // 2
PITCH = 72
F32 = jnp.float32
BF16 = jnp.bfloat16
MESH = pl.DeviceIdType.MESH
NT = (((1,), (1,)), ((), ()))
NN = (((1,), (0,)), ((), ()))
LEVELS = (4, 8, 4)
CHUNKS = 2
PIECE = 4
GROUPS = 2 * KL + 3


def split(x):
    hi = x.astype(BF16)
    return hi, (x - hi.astype(F32)).astype(BF16)


def mm(a, b, dims):
    return lax.dot_general(a, b, dims, preferred_element_type=F32)


def dot3(x, w, dims=NN):
    m = x.shape[0]
    xh, xl = split(x)
    wh, wl = split(w)
    if dims == NT and w.shape[1] <= 128:
        both = jnp.concatenate(
            [jnp.concatenate([xh, xh], axis=1), jnp.concatenate([xl, xl], axis=1)], axis=0
        )
        both = mm(both, jnp.concatenate([wh, wl], axis=1), dims)
        return both[:m] + both[m:]
    both = jnp.concatenate([xh, xl], axis=0)
    if dims == NN and w.shape[1] % 128 == 0:
        n = w.shape[1]
        both = mm(both, jnp.concatenate([wh, wl], axis=1), dims)
        return both[:m, :n] + both[m:, :n] + both[:m, n:]
    both = mm(both, wh, dims)
    return both[:m] + both[m:] + mm(xh, wl, dims)


def dot2(x, w, dims=NN):
    m = x.shape[0]
    xh, xl = split(x)
    both = mm(jnp.concatenate([xh, xl], axis=0), w, dims)
    return both[:m] + both[m:]


def iota(shape, axis):
    return lax.broadcasted_iota(jnp.int32, shape, axis)


def lower_half():
    return iota((1, 128), 1) < U


def swap_halves(x):
    return pltpu.roll(x, U, axis=1)


def one_hot(lcols, ucols, active, half):
    e = iota((KL, 256), 0)
    group = iota((KL, 256), 1) // 8
    low = lcols[...].astype(F32).astype(BF16)
    up = ucols[...].astype(F32).astype(BF16)
    listed = mm(low, (group == e).astype(BF16), NN) + mm(up, (group == e + KL).astype(BF16), NN)
    lane = iota((1, 256), 1)
    group = lane // 8
    k = lane % 8 + 8 * half
    own = iota((NB, 256), 0) == iota((NB, 256), 1) % 8 + 8 * half
    target = jnp.sum(jnp.where(own, listed, 0.0), axis=0, keepdims=True).astype(jnp.int32)
    target = jnp.where(group == 2 * KL, k, target)
    target = jnp.where(group == 2 * KL + 1, 16, target)
    target = jnp.where(group == 2 * KL + 2, 17, target)
    target = jnp.where((group < GROUPS) & ((group == 2 * KL) | (k < active)), target, -1)
    r = iota((144, 256), 0)
    second = (r >= 72).astype(jnp.int32)
    column = 2 * (r // 8) - 17 * second
    return jnp.where((column == target) & (lane % 8 == r % 8), 1.0, 0.0).astype(BF16)


def assemble(sources, few, lcols, ucols, active, stack, panel, sems, hots, raw, fence):
    width = U * U // CHUNKS
    copies = {}
    for copy in few:
        copy.start()
    for half in range(2):
        for q in range(CHUNKS):
            lanes = pl.ds(width * q, width)
            row, first = [], 0
            for n, src in enumerate(sources):
                count = src.shape[0]
                copy = pltpu.make_async_copy(
                    src.at[:, pl.ds(8 * half, 8), lanes],
                    stack.at[half, pl.ds(first, count), :, lanes],
                    sems.at[n, half * CHUNKS + q],
                )
                copy.start()
                row.append(copy)
                first += count
            copies[half, q] = row
    stack[:, GROUPS:] = jnp.zeros((2, 32 - GROUPS, 8, U * U), BF16)
    low = lower_half()
    tiles = 16 // CHUNKS
    for copy in few:
        copy.wait()

    for half in range(2):
        hots[half] = one_hot(lcols, ucols, active, half)
    pieces = [(half, first) for half in range(2) for first in range(0, 16, PIECE)]
    for n in range(len(pieces) + 1):
        if n < len(pieces) and pieces[n][1] % tiles == 0:
            for copy in copies[pieces[n][0], pieces[n][1] // tiles]:
                copy.wait()

        @fence
        def _():
            if n < len(pieces):
                half, first = pieces[n]
                for t in range(PIECE):
                    lanes = pl.ds(256 * (first + t), 256)
                    raw[n % 2, t] = mm(hots[half], stack[half, :, :, lanes].reshape(256, 256), NN)
            if n:
                half, first = pieces[n - 1]
                for t in range(PIECE):
                    for s in range(2):
                        even = raw[(n - 1) % 2, t, 0:72, pl.ds(128 * s, 128)]
                        odd = raw[(n - 1) % 2, t, 72:144, pl.ds(128 * s, 128)]
                        i = 4 * (first + t) + 2 * s
                        panel[half][pl.ds(i, 72, stride=PITCH), :] = jnp.where(low, even, swap_halves(odd))
                        panel[half][pl.ds(i + 1, 72, stride=PITCH), :] = jnp.where(low, swap_halves(even), odd)


def block(panel, c2, k):
    return panel[k // 8][pl.ds((c2 * 8 + k % 8) * PITCH, U), :]


def column_blocks(panel, c2, first, last):
    return jnp.concatenate([block(panel, c2, k) for k in range(first, last)], axis=0)


def group_blocks(panel, s, first, last):
    return jnp.concatenate([column_blocks(panel, 2 * s + d, first, last) for d in range(2)], axis=1)


def operators(panel, ops, fops):
    low = lower_half()
    zeros = jnp.zeros((128, 128), F32)
    eye = jnp.where(iota((128, 128), 0) == iota((128, 128), 1), 1.0, 0.0)
    evens = [block(panel, c, 2 * c) for c in range(8)]
    odds = [block(panel, c, 2 * c + 1) for c in range(8)]
    fs = [eye - jnp.concatenate([zeros[:U], jnp.where(low, odd, 0.0)], axis=0) for odd in odds]
    lowers = [dot3(fs[2 * s + 1], column_blocks(panel, 2 * s, 4 * s + 2, 4 * s + 4)) for s in range(4)]
    inners = [dot3(even[:, :U], jnp.where(low, 0.0, even)) for even in evens]
    rights = [jnp.where(low, 0.0, odd) for odd in odds]
    inners = [swap_halves(inner)[:, :U] for inner in inners]
    inners = [dot2(inner, right.astype(BF16)) for inner, right in zip(inners, rights)]
    lowers = [dot3(lowers[s], fs[2 * s]) for s in range(4)]
    bs = [
        jnp.concatenate([jnp.where(low, even, -inner), right], axis=0)
        for even, inner, right in zip(evens, inners, rights)
    ]
    uppers = [dot3(bs[2 * s], column_blocks(panel, 2 * s + 1, 4 * s, 4 * s + 2)) for s in range(4)]
    for s in range(4):
        fops[s, 0:128, 0:128] = fs[2 * s]
        fops[s, 0:128, 128:256] = zeros
        fops[s, 128:256, 0:128] = -lowers[s]
        fops[s, 128:256, 128:256] = fs[2 * s + 1]
    uppers = [dot3(uppers[s], bs[2 * s + 1]) for s in range(4)]
    for s in range(4):
        ops[s, 0:128, 0:128] = bs[2 * s]
        ops[s, 0:128, 128:256] = -uppers[s]
        ops[s, 128:256, 0:128] = zeros
        ops[s, 128:256, 128:256] = bs[2 * s + 1]


def forward(rhs, active, panel, work, gt, hacc, ops, fops):
    low = lower_half()
    eye = (iota((128, 128), 0) == iota((128, 128), 1)).astype(BF16)
    last = jnp.zeros((N1, 128), F32)
    hacc[...] = jnp.where(iota((U, NB * U), 0) == iota((U, NB * U), 1), 1.0, 0.0)
    live = (iota((1, NB * U), 1) // U) < active
    work[0:R, :] = jnp.where(live, rhs[...], 0.0)
    work[R:, :] = -mm(eye, column_blocks(panel, 8, 0, NB).astype(BF16), NT)
    operators(panel, ops, fops)
    for s in range(4):
        here = pl.ds(256 * s, 256)
        x = dot3(work[0:N1, here], fops[s], NT)
        g = dot3(hacc[:, here], ops[s])
        if s < 3:
            rest = pl.ds(256 * (s + 1), 256 * (3 - s))
            work[0:N1, rest] -= dot3(x, group_blocks(panel, s, 4 * s + 4, NB), NT)
            weights = [group_blocks(panel, d, 4 * s, 4 * s + 4) for d in range(s + 1, 4)]
            hacc[:, rest] -= dot3(g, jnp.concatenate(weights, axis=1))
        work[0:N1, here] = x
        gt[:, here] = g
        for d in range(2):
            mine = 4 * s + 2 * d + jnp.where(low, 0, 1) == active - 1
            last = last + jnp.where(mine, x[:, 128 * d : 128 * d + 128], 0.0)
    boundary = last + swap_halves(last)
    weights = jnp.concatenate([jnp.zeros((U, NB * U), F32), gt[...]], axis=0)
    z0 = dot3(work[...], weights, NT)
    return jnp.concatenate([jnp.where(low, boundary, z0[:N1]), z0[N1:]], axis=0)


def backward_step(s, panel, work, zbuf, ops):
    here = pl.ds(256 * s, 256)
    z = dot3(work[:, here], ops[s], NT)
    zbuf[:, here] = z
    if s:
        work[:, pl.ds(0, 256 * s)] -= dot3(z, group_blocks(panel, s, 0, 4 * s), NT)


def unpack(m):
    low = lower_half()
    d = m[N1:]
    return jnp.concatenate(
        [m[:N1], jnp.where(low, 0.0, swap_halves(d)), jnp.where(low, 0.0, d)], axis=0
    )


def pack(m):
    top, bottom = m[N1 : N1 + U // 2], m[N1 + U // 2 :]
    return jnp.concatenate([m[:N1], jnp.where(lower_half(), swap_halves(top), bottom)], axis=0)


def compose(left, right):
    t = dot3(left[:N1, :U], right[R:N1])
    t = jnp.concatenate([t[:R] + right[:R], t[R:]], axis=0)
    weights = jnp.concatenate([jnp.zeros((U, 128), F32), left[N1:]], axis=0)
    s = dot3(jnp.concatenate([t, right[N1:]], axis=0), weights)
    return jnp.concatenate([jnp.where(lower_half(), t, s[:N1] + left[:N1]), s[N1:]], axis=0)


def identity_map():
    r = iota((N2, 128), 0)
    lane = iota((N2, 128), 1)
    one = ((r >= R) & (r < N1) & (lane == r - R)) | ((r >= N1) & (lane == r - N1 + U))
    return jnp.where(one, 1.0, 0.0)


def narrow(right, sibling, before, after):
    c = compose(jnp.where(right, sibling, after), jnp.where(right, before, sibling))
    return jnp.where(right, c, before), jnp.where(right, after, c)


def kernel(
    levels, rhs_in, lower, upper, diag, llow, lup, lcols_in, ucols_in, counts, *rest
):
    if levels is None:
        maps, zout, stack, panel0, panel1, work, zbuf, gt, hacc, ops, fops, in_sems, rhs, lcols, ucols, few_sems, hots, raw = rest
        few = [
            pltpu.make_async_copy(src, dst, few_sems.at[n])
            for n, (src, dst) in enumerate(((lcols_in, lcols), (ucols_in, ucols), (rhs_in, rhs)))
        ]
        active = counts[0]
        panel = (panel0, panel1)
        fence = lambda f: f()
        assemble((lower, upper, diag, llow, lup), few, lcols, ucols, active, stack, panel, in_sems, hots, raw, fence)
        maps[...] = pack(forward(rhs, active, panel, work, gt, hacc, ops, fops))
        for s in reversed(range(4)):
            backward_step(s, panel, work, zout, ops)
        return
    (
        out, stack, panel0, panel1, work, zbuf, gt, hacc, ops, fops, in_sems, rhs, lcols, ucols, few_sems, hots, raw,
        b_core, b_y, b_z, b_x, b_half, y_pairs, z_pairs, z_near, sides,
        s_core, r_core, s_half, r_half, s_sib, r_sib, s_y, r_y, s_z, r_z, s_x, r_x,
    ) = rest
    nx, nz, ny = levels
    chain = lax.axis_index("chain")
    side = lax.axis_index("side")
    y = chain % ny
    zz = (chain // ny) % nz
    x = chain // (ny * nz)

    def at_core():
        return (chain, 1 - side)

    def at_y(k):
        return (chain - y + (y + k) % ny, side)

    def at_z(k, core):
        return (chain - zz * ny + ((zz + k) % nz) * ny, core)

    def at_x(k):
        return (((x + k) % nx) * (ny * nz) + chain % (ny * nz), side)

    peers = [at_core()]
    peers += [at_y(k) for k in range(1, ny)]
    peers += [at_z(k, core) for k in range(1, nz) for core in range(2)]
    peers += [at_x(k) for k in range(1, nx)]
    barrier = pltpu.get_barrier_semaphore()
    for peer in peers:
        pl.semaphore_signal(barrier, inc=1, device_id=peer, device_id_type=MESH)

    def remote(src, dst, send, recv, peer):
        return pltpu.make_async_remote_copy(
            src_ref=src, dst_ref=dst, send_sem=send, recv_sem=recv, device_id=peer, device_id_type=MESH
        )

    def ring(buf, index, count, peer_of, send, recv):
        copies = []
        for k in sorted(range(1, count), key=lambda k: -min(k, count - k)):
            copies.append(remote(buf.at[index], buf.at[index], send.at[k - 1], recv.at[k - 1], peer_of(k)))
        for copy in copies:
            copy.start()
        return copies

    def finish(copies):
        for copy in copies:
            copy.wait()

    half = nz // 2
    home = zz // half
    order = sorted(range(1, nz), key=lambda k: -min(k, nz - k))

    def z_copy(k):
        return remote(b_z.at[zz], b_z.at[zz], s_z.at[k - 1], r_z.at[k - 1], at_z(k, home))

    def z_start():
        for k in order:
            @pl.when(side == (0 if k <= half else 1))
            def _():
                z_copy(k).start()

    def z_finish():
        for k in order:
            @pl.when(((zz + nz - k) % nz) // half == side)
            def _():
                z_copy(k).wait_recv()
        for k in order:
            @pl.when(side == (0 if k <= half else 1))
            def _():
                z_copy(k).wait_send()

    few = [
        pltpu.make_async_copy(src, dst, few_sems.at[n])
        for n, (src, dst) in enumerate(((lcols_in, lcols), (ucols_in, ucols), (rhs_in, rhs)))
    ]
    active = counts[0]
    panel = (panel0, panel1)
    fence = pl.when(chain + zz < 777)
    assemble((lower, upper, diag, llow, lup), few, lcols, ucols, active, stack, panel, in_sems, hots, raw, fence)
    b_core[side] = pack(forward(rhs, active, panel, work, gt, hacc, ops, fops))
    pl.semaphore_wait(barrier, len(peers))

    core = remote(b_core.at[side], b_core.at[side], s_core, r_core, at_core())
    core.start()
    core.wait()

    @fence
    def _():
        b_y[y] = pack(compose(unpack(b_core[0]), unpack(b_core[1])))

    ys = ring(b_y, y, ny, at_y, s_y, r_y)

    @fence
    def _():
        for s in (3, 2):
            backward_step(s, panel, work, zbuf, ops)

    finish(ys)

    @fence
    def _():
        nodes = [compose(unpack(b_y[i]), unpack(b_y[i + 1])) for i in range(0, ny, 2)]
        for i, node in enumerate(nodes):
            y_pairs[i] = node
        b_z[zz] = pack(compose(*nodes))

    z_start()

    @fence
    def _():
        for s in (1, 0):
            backward_step(s, panel, work, zbuf, ops)

    @fence
    def _():
        before = after = identity_map()
        before, after = narrow(side == 1, unpack(b_core[1 - side]), before, after)
        before, after = narrow(y % 2 == 1, unpack(b_y[y + 1 - 2 * (y % 2)]), before, after)
        before, after = narrow(y // 2 == 1, y_pairs[1 - y // 2], before, after)
        sides[0] = before
        sides[1] = after

    z_finish()
    first = side * half
    sibling = zz + 1 - 2 * (zz % 2)

    @fence
    def _():
        nodes = [compose(unpack(b_z[first + i]), unpack(b_z[first + i + 1])) for i in range(0, half, 2)]
        for i, node in enumerate(nodes):
            z_pairs[i] = node
        b_half[side] = pack(compose(*nodes))

    swap = remote(b_half.at[side], b_half.at[side], s_half, r_half, at_core())
    swap.start()
    leaf = remote(b_z.at[sibling], b_z.at[sibling], s_sib.at[0], r_sib.at[0], at_core())
    near = remote(z_near, z_near, s_sib.at[1], r_sib.at[1], at_core())

    @pl.when(home == side)
    def _():
        z_near[...] = z_pairs[1 - (zz % half) // 2]
        leaf.start()
        near.start()

    swap.wait()

    @fence
    def _():
        b_x[x] = pack(compose(unpack(b_half[0]), unpack(b_half[1])))

    xs = ring(b_x, x, nx, at_x, s_x, r_x)

    @pl.when(home == side)
    def _():
        leaf.wait_send()
        near.wait_send()

    @pl.when(home != side)
    def _():
        leaf.wait_recv()
        near.wait_recv()

    @fence
    def _():
        before, after = sides[0], sides[1]
        before, after = narrow(zz % 2 == 1, unpack(b_z[sibling]), before, after)
        before, after = narrow((zz % half) // 2 == 1, z_near[...], before, after)
        before, after = narrow(home == 1, unpack(b_half[1 - home]), before, after)
        sides[0] = before
        sides[1] = after

    finish(xs)

    t = b_x[0, 0:R]
    p = jnp.zeros((R, U), F32)
    ends = [t]
    for j in range(1, nx):
        p = jnp.where(x == j, t[:, :U], p)
        t = dot3(t[:, :U], b_x[j, R:N1]) + b_x[j, 0:R]
        ends.append(t)
    q_run = ends[nx - 1][:, U:]
    q = jnp.zeros((R, U), F32)
    for j in reversed(range(nx - 1)):
        q = jnp.where(x == j, q_run, q)
        if j:
            q_run = dot3(q_run, unpack(b_x[j])[N1:, U:]) + ends[j][:, U:]
    own = unpack(b_core[side])
    before, after = sides[0], sides[1]
    p = dot3(p, before[R:N1, :U]) + before[:R, :U]
    t = dot3(p, own[R:N1, :U]) + own[:R, :U]
    t = dot3(t, after[R:N1]) + after[:R]
    q = t[:, U:] + dot3(q, after[N1:, U:])
    out[...] = zbuf[0:R, :] + dot3(jnp.concatenate([p, q], axis=1), zbuf[R:, :])


def local(levels, interpret, rhs, lower, lcols, upper, ucols, diag, llow, lup, counts):
    vmem = pl.BlockSpec(memory_space=pltpu.VMEM)
    anywhere = pl.BlockSpec(memory_space=pl.ANY)
    dma = pltpu.SemaphoreType.DMA
    lower = jnp.transpose(lower, (1, 0, 2))
    upper = jnp.transpose(upper, (1, 0, 2))
    diag, llow, lup = diag[None], llow[None], lup[None]
    cols = NB * U
    lcols, ucols, rhs = (pltpu.with_memory_space_constraint(v, pltpu.HBM) for v in (lcols, ucols, rhs))
    lower, upper, diag, llow, lup = (pltpu.with_memory_space_constraint(v, pltpu.HBM) for v in (lower, upper, diag, llow, lup))
    scratch = [
        pltpu.VMEM((2, 32, 8, U * U), BF16),
        pltpu.VMEM((72 * PITCH, 128), F32),
        pltpu.VMEM((72 * PITCH, 128), F32),
        pltpu.VMEM((N2, cols), F32),
        pltpu.VMEM((N2, cols), F32),
        pltpu.VMEM((U, cols), F32),
        pltpu.VMEM((U, cols), F32),
        pltpu.VMEM((4, 256, 256), F32),
        pltpu.VMEM((4, 256, 256), F32),
        dma((5, 2 * CHUNKS)),
        pltpu.VMEM((R, cols), F32),
        pltpu.VMEM((NB, KL), jnp.int32),
        pltpu.VMEM((NB, KL), jnp.int32),
        dma((3,)),
        pltpu.VMEM((2, 144, 256), BF16),
        pltpu.VMEM((2, PIECE, 144, 256), F32),
    ]
    if levels is None:
        outs = (jax.ShapeDtypeStruct((PACKED, 128), F32), jax.ShapeDtypeStruct((N2, cols), F32))
        params = pltpu.CompilerParams(vmem_limit_bytes=48000000)
    else:
        nx, nz, ny = levels
        outs = jax.ShapeDtypeStruct((R, cols), F32)
        scratch += [pltpu.VMEM((n, PACKED, 128), F32) for n in (2, ny, nz, nx, 2)]
        scratch += [pltpu.VMEM(m + (N2, 128), F32) for m in ((ny // 2,), (nz // 4,), (), (2,))]
        scratch += [dma] * 4 + [dma((2,))] * 2 + [dma((n - 1,)) for n in (ny, ny, nz, nz, nx, nx)]
        params = pltpu.CompilerParams(
            collective_id=0, has_side_effects=True, vmem_limit_bytes=48000000
        )
    return pl.pallas_call(
        functools.partial(kernel, levels),
        out_shape=outs,
        in_specs=[anywhere] * 8 + [pl.BlockSpec(memory_space=pltpu.SMEM)],
        out_specs=jax.tree.map(lambda _: vmem, outs),
        scratch_shapes=scratch,
        compiler_params=params,
        interpret=interpret,
        name="ilu_apply",
    )(rhs, lower, upper, diag, llow, lup, lcols, ucols, counts)


def solution(mesh, levels=LEVELS):
    both = ("chain", "side")
    return jax.shard_map(
        functools.partial(local, levels, False),
        mesh=mesh,
        in_specs=(
            P(None, both),
            P(both, None, None),
            P(both, None),
            P(both, None, None),
            P(both, None),
            P(both, None),
            P(both, None),
            P(both, None),
            P(both),
        ),
        out_specs=P(None, both),
        check_vma=False,
    )
```

```python
import functools

import jax
import jax.numpy as jnp
from jax import lax
from jax.experimental import pallas as pl
from jax.experimental.pallas import tpu as pltpu
from jax.sharding import PartitionSpec as P

U = 64
R = 8
NB = 16
KL = 13
N1 = R + U
N2 = R + 2 * U
PACKED = R + U + U // 2
PITCH = 72
F32 = jnp.float32
BF16 = jnp.bfloat16
MESH = pl.DeviceIdType.MESH
NT = (((1,), (1,)), ((), ()))
NN = (((1,), (0,)), ((), ()))
LEVELS = (4, 8, 4)
CHUNKS = 2
PIECE = 4
GROUPS = 2 * KL + 3


def split(x):
    hi = x.astype(BF16)
    return hi, (x - hi.astype(F32)).astype(BF16)


def mm(a, b, dims):
    return lax.dot_general(a, b, dims, preferred_element_type=F32)


def dot3(x, w, dims=NN):
    m = x.shape[0]
    xh, xl = split(x)
    wh, wl = split(w)
    if dims == NT and w.shape[1] <= 128:
        both = jnp.concatenate(
            [jnp.concatenate([xh, xh], axis=1), jnp.concatenate([xl, xl], axis=1)], axis=0
        )
        both = mm(both, jnp.concatenate([wh, wl], axis=1), dims)
        return both[:m] + both[m:]
    both = jnp.concatenate([xh, xl], axis=0)
    if dims == NN and w.shape[1] % 128 == 0:
        n = w.shape[1]
        both = mm(both, jnp.concatenate([wh, wl], axis=1), dims)
        return both[:m, :n] + both[m:, :n] + both[:m, n:]
    both = mm(both, wh, dims)
    return both[:m] + both[m:] + mm(xh, wl, dims)


def dot2(x, w, dims=NN):
    m = x.shape[0]
    xh, xl = split(x)
    both = mm(jnp.concatenate([xh, xl], axis=0), w, dims)
    return both[:m] + both[m:]


def iota(shape, axis):
    return lax.broadcasted_iota(jnp.int32, shape, axis)


def lower_half():
    return iota((1, 128), 1) < U


def swap_halves(x):
    return pltpu.roll(x, U, axis=1)


def one_hot(lcols, ucols, active, half):
    e = iota((KL, 256), 0)
    group = iota((KL, 256), 1) // 8
    low = lcols[...].astype(F32).astype(BF16)
    up = ucols[...].astype(F32).astype(BF16)
    listed = mm(low, (group == e).astype(BF16), NN) + mm(up, (group == e + KL).astype(BF16), NN)
    lane = iota((1, 256), 1)
    group = lane // 8
    k = lane % 8 + 8 * half
    own = iota((NB, 256), 0) == iota((NB, 256), 1) % 8 + 8 * half
    target = jnp.sum(jnp.where(own, listed, 0.0), axis=0, keepdims=True).astype(jnp.int32)
    target = jnp.where(group == 2 * KL, k, target)
    target = jnp.where(group == 2 * KL + 1, 16, target)
    target = jnp.where(group == 2 * KL + 2, 17, target)
    target = jnp.where((group < GROUPS) & ((group == 2 * KL) | (k < active)), target, -1)
    r = iota((144, 256), 0)
    second = (r >= 72).astype(jnp.int32)
    column = 2 * (r // 8) - 17 * second
    return jnp.where((column == target) & (lane % 8 == r % 8), 1.0, 0.0).astype(BF16)


def assemble(sources, few, lcols, ucols, active, stack, panel, sems, hots, raw, fence):
    width = U * U // CHUNKS
    copies = {}
    for copy in few:
        copy.start()
    for half in range(2):
        for q in range(CHUNKS):
            lanes = pl.ds(width * q, width)
            row, first = [], 0
            for n, src in enumerate(sources):
                count = src.shape[0]
                copy = pltpu.make_async_copy(
                    src.at[:, pl.ds(8 * half, 8), lanes],
                    stack.at[half, pl.ds(first, count), :, lanes],
                    sems.at[n, half * CHUNKS + q],
                )
                copy.start()
                row.append(copy)
                first += count
            copies[half, q] = row
    stack[:, GROUPS:] = jnp.zeros((2, 32 - GROUPS, 8, U * U), BF16)
    low = lower_half()
    tiles = 16 // CHUNKS
    for copy in few:
        copy.wait()

    for half in range(2):
        hots[half] = one_hot(lcols, ucols, active, half)
    pieces = [(half, first) for half in range(2) for first in range(0, 16, PIECE)]
    for n in range(len(pieces) + 1):
        if n < len(pieces) and pieces[n][1] % tiles == 0:
            for copy in copies[pieces[n][0], pieces[n][1] // tiles]:
                copy.wait()

        @fence
        def _():
            if n < len(pieces):
                half, first = pieces[n]
                for t in range(PIECE):
                    lanes = pl.ds(256 * (first + t), 256)
                    raw[n % 2, t] = mm(hots[half], stack[half, :, :, lanes].reshape(256, 256), NN)
            if n:
                half, first = pieces[n - 1]
                for t in range(PIECE):
                    for s in range(2):
                        even = raw[(n - 1) % 2, t, 0:72, pl.ds(128 * s, 128)]
                        odd = raw[(n - 1) % 2, t, 72:144, pl.ds(128 * s, 128)]
                        i = 4 * (first + t) + 2 * s
                        panel[half][pl.ds(i, 72, stride=PITCH), :] = jnp.where(low, even, swap_halves(odd))
                        panel[half][pl.ds(i + 1, 72, stride=PITCH), :] = jnp.where(low, swap_halves(even), odd)


def block(panel, c2, k):
    return panel[k // 8][pl.ds((c2 * 8 + k % 8) * PITCH, U), :]


def column_blocks(panel, c2, first, last):
    return jnp.concatenate([block(panel, c2, k) for k in range(first, last)], axis=0)


def group_blocks(panel, s, first, last):
    return jnp.concatenate([column_blocks(panel, 2 * s + d, first, last) for d in range(2)], axis=1)


def operators(panel, ops, fops):
    low = lower_half()
    zeros = jnp.zeros((128, 128), F32)
    eye = jnp.where(iota((128, 128), 0) == iota((128, 128), 1), 1.0, 0.0)
    evens = [block(panel, c, 2 * c) for c in range(8)]
    odds = [block(panel, c, 2 * c + 1) for c in range(8)]
    fs = [eye - jnp.concatenate([zeros[:U], jnp.where(low, odd, 0.0)], axis=0) for odd in odds]
    lowers = [dot3(fs[2 * s + 1], column_blocks(panel, 2 * s, 4 * s + 2, 4 * s + 4)) for s in range(4)]
    inners = [dot3(even[:, :U], jnp.where(low, 0.0, even)) for even in evens]
    rights = [jnp.where(low, 0.0, odd) for odd in odds]
    inners = [swap_halves(inner)[:, :U] for inner in inners]
    inners = [dot2(inner, right.astype(BF16)) for inner, right in zip(inners, rights)]
    lowers = [dot3(lowers[s], fs[2 * s]) for s in range(4)]
    bs = [
        jnp.concatenate([jnp.where(low, even, -inner), right], axis=0)
        for even, inner, right in zip(evens, inners, rights)
    ]
    uppers = [dot3(bs[2 * s], column_blocks(panel, 2 * s + 1, 4 * s, 4 * s + 2)) for s in range(4)]
    for s in range(4):
        fops[s, 0:128, 0:128] = fs[2 * s]
        fops[s, 0:128, 128:256] = zeros
        fops[s, 128:256, 0:128] = -lowers[s]
        fops[s, 128:256, 128:256] = fs[2 * s + 1]
    uppers = [dot3(uppers[s], bs[2 * s + 1]) for s in range(4)]
    for s in range(4):
        ops[s, 0:128, 0:128] = bs[2 * s]
        ops[s, 0:128, 128:256] = -uppers[s]
        ops[s, 128:256, 0:128] = zeros
        ops[s, 128:256, 128:256] = bs[2 * s + 1]


def forward(rhs, active, panel, work, gt, hacc, ops, fops):
    low = lower_half()
    eye = (iota((128, 128), 0) == iota((128, 128), 1)).astype(BF16)
    last = jnp.zeros((N1, 128), F32)
    hacc[...] = jnp.where(iota((U, NB * U), 0) == iota((U, NB * U), 1), 1.0, 0.0)
    live = (iota((1, NB * U), 1) // U) < active
    work[0:R, :] = jnp.where(live, rhs[...], 0.0)
    work[R:, :] = -mm(eye, column_blocks(panel, 8, 0, NB).astype(BF16), NT)
    operators(panel, ops, fops)
    for s in range(4):
        here = pl.ds(256 * s, 256)
        x = dot3(work[0:N1, here], fops[s], NT)
        g = dot3(hacc[:, here], ops[s])
        if s < 3:
            rest = pl.ds(256 * (s + 1), 256 * (3 - s))
            work[0:N1, rest] -= dot3(x, group_blocks(panel, s, 4 * s + 4, NB), NT)
            weights = [group_blocks(panel, d, 4 * s, 4 * s + 4) for d in range(s + 1, 4)]
            hacc[:, rest] -= dot3(g, jnp.concatenate(weights, axis=1))
        work[0:N1, here] = x
        gt[:, here] = g
        for d in range(2):
            mine = 4 * s + 2 * d + jnp.where(low, 0, 1) == active - 1
            last = last + jnp.where(mine, x[:, 128 * d : 128 * d + 128], 0.0)
    boundary = last + swap_halves(last)
    weights = jnp.concatenate([jnp.zeros((U, NB * U), F32), gt[...]], axis=0)
    z0 = dot3(work[...], weights, NT)
    return jnp.concatenate([jnp.where(low, boundary, z0[:N1]), z0[N1:]], axis=0)


def backward_step(s, panel, work, zbuf, ops):
    here = pl.ds(256 * s, 256)
    z = dot3(work[:, here], ops[s], NT)
    zbuf[:, here] = z
    if s:
        work[:, pl.ds(0, 256 * s)] -= dot3(z, group_blocks(panel, s, 0, 4 * s), NT)


def unpack(m):
    low = lower_half()
    d = m[N1:]
    return jnp.concatenate(
        [m[:N1], jnp.where(low, 0.0, swap_halves(d)), jnp.where(low, 0.0, d)], axis=0
    )


def pack(m):
    top, bottom = m[N1 : N1 + U // 2], m[N1 + U // 2 :]
    return jnp.concatenate([m[:N1], jnp.where(lower_half(), swap_halves(top), bottom)], axis=0)


def compose(left, right):
    t = dot3(left[:N1, :U], right[R:N1])
    t = jnp.concatenate([t[:R] + right[:R], t[R:]], axis=0)
    weights = jnp.concatenate([jnp.zeros((U, 128), F32), left[N1:]], axis=0)
    s = dot3(jnp.concatenate([t, right[N1:]], axis=0), weights)
    return jnp.concatenate([jnp.where(lower_half(), t, s[:N1] + left[:N1]), s[N1:]], axis=0)


def identity_map():
    r = iota((N2, 128), 0)
    lane = iota((N2, 128), 1)
    one = ((r >= R) & (r < N1) & (lane == r - R)) | ((r >= N1) & (lane == r - N1 + U))
    return jnp.where(one, 1.0, 0.0)


def narrow(right, sibling, before, after):
    c = compose(jnp.where(right, sibling, after), jnp.where(right, before, sibling))
    return jnp.where(right, c, before), jnp.where(right, after, c)


def kernel(
    levels, rhs_in, lower, upper, diag, llow, lup, lcols_in, ucols_in, counts, *rest
):
    if levels is None:
        maps, zout, stack, panel0, panel1, work, zbuf, gt, hacc, ops, fops, in_sems, rhs, lcols, ucols, few_sems, hots, raw = rest
        few = [
            pltpu.make_async_copy(src, dst, few_sems.at[n])
            for n, (src, dst) in enumerate(((lcols_in, lcols), (ucols_in, ucols), (rhs_in, rhs)))
        ]
        active = counts[0]
        panel = (panel0, panel1)
        fence = lambda f: f()
        assemble((lower, upper, diag, llow, lup), few, lcols, ucols, active, stack, panel, in_sems, hots, raw, fence)
        maps[...] = pack(forward(rhs, active, panel, work, gt, hacc, ops, fops))
        for s in reversed(range(4)):
            backward_step(s, panel, work, zout, ops)
        return
    (
        out, stack, panel0, panel1, work, zbuf, gt, hacc, ops, fops, in_sems, rhs, lcols, ucols, few_sems, hots, raw,
        b_core, b_y, b_z, b_x, b_half, y_pairs, z_pairs, z_near, sides,
        s_core, r_core, s_half, r_half, s_sib, r_sib, s_y, r_y, s_z, r_z, s_x, r_x,
    ) = rest
    nx, nz, ny = levels
    chain = lax.axis_index("chain")
    side = lax.axis_index("side")
    y = chain % ny
    zz = (chain // ny) % nz
    x = chain // (ny * nz)

    def at_core():
        return (chain, 1 - side)

    def at_y(k):
        return (chain - y + (y + k) % ny, side)

    def at_z(k, core):
        return (chain - zz * ny + ((zz + k) % nz) * ny, core)

    def at_x(k):
        return (((x + k) % nx) * (ny * nz) + chain % (ny * nz), side)

    peers = [at_core()]
    peers += [at_y(k) for k in range(1, ny)]
    peers += [at_z(k, core) for k in range(1, nz) for core in range(2)]
    peers += [at_x(k) for k in range(1, nx)]
    barrier = pltpu.get_barrier_semaphore()
    for peer in peers:
        pl.semaphore_signal(barrier, inc=1, device_id=peer, device_id_type=MESH)

    def remote(src, dst, send, recv, peer):
        return pltpu.make_async_remote_copy(
            src_ref=src, dst_ref=dst, send_sem=send, recv_sem=recv, device_id=peer, device_id_type=MESH
        )

    def ring(buf, index, peer_of, send, recv):
        def copy(slot, k, hop):
            part = buf.at[slot % 4]
            return remote(part, part, send.at[k - 1], recv.at[k - 1], peer_of(hop))

        far, ahead, behind = (copy(index, k, k) for k in (2, 1, 3))

        @pl.when(side == 0)
        def _():
            far.start()

        behind.start()
        ahead.start()
        return far, ahead, behind, copy(index + 1, 2, 3)

    def finish(copies):
        far, ahead, behind, onward = copies
        behind.wait_recv()

        @pl.when(side == 1)
        def _():
            onward.start()

        behind.wait_send()
        ahead.wait()

        @pl.when(side == 0)
        def _():
            far.wait()

        @pl.when(side == 1)
        def _():
            onward.wait()

    half = nz // 2
    home = zz // half
    order = sorted(range(1, nz), key=lambda k: -min(k, nz - k))

    def z_copy(k):
        return remote(b_z.at[zz], b_z.at[zz], s_z.at[k - 1], r_z.at[k - 1], at_z(k, home))

    def z_start():
        for k in order:
            @pl.when(side == (0 if k <= half else 1))
            def _():
                z_copy(k).start()

    def z_finish():
        for k in order:
            @pl.when(((zz + nz - k) % nz) // half == side)
            def _():
                z_copy(k).wait_recv()
        for k in order:
            @pl.when(side == (0 if k <= half else 1))
            def _():
                z_copy(k).wait_send()

    few = [
        pltpu.make_async_copy(src, dst, few_sems.at[n])
        for n, (src, dst) in enumerate(((lcols_in, lcols), (ucols_in, ucols), (rhs_in, rhs)))
    ]
    active = counts[0]
    panel = (panel0, panel1)
    fence = pl.when(chain + zz < 777)
    assemble((lower, upper, diag, llow, lup), few, lcols, ucols, active, stack, panel, in_sems, hots, raw, fence)
    b_core[side] = pack(forward(rhs, active, panel, work, gt, hacc, ops, fops))
    pl.semaphore_wait(barrier, len(peers))

    core = remote(b_core.at[side], b_core.at[side], s_core, r_core, at_core())
    core.start()
    core.wait()

    @fence
    def _():
        b_y[y] = pack(compose(unpack(b_core[0]), unpack(b_core[1])))

    ys = ring(b_y, y, at_y, s_y, r_y)

    @fence
    def _():
        for s in (3, 2):
            backward_step(s, panel, work, zbuf, ops)

    finish(ys)

    @fence
    def _():
        nodes = [compose(unpack(b_y[i]), unpack(b_y[i + 1])) for i in range(0, ny, 2)]
        for i, node in enumerate(nodes):
            y_pairs[i] = node
        b_z[zz] = pack(compose(*nodes))

    z_start()

    @fence
    def _():
        for s in (1, 0):
            backward_step(s, panel, work, zbuf, ops)

    @fence
    def _():
        before = after = identity_map()
        before, after = narrow(side == 1, unpack(b_core[1 - side]), before, after)
        before, after = narrow(y % 2 == 1, unpack(b_y[y + 1 - 2 * (y % 2)]), before, after)
        before, after = narrow(y // 2 == 1, y_pairs[1 - y // 2], before, after)
        sides[0] = before
        sides[1] = after

    z_finish()
    first = side * half
    sibling = zz + 1 - 2 * (zz % 2)

    @fence
    def _():
        nodes = [compose(unpack(b_z[first + i]), unpack(b_z[first + i + 1])) for i in range(0, half, 2)]
        for i, node in enumerate(nodes):
            z_pairs[i] = node
        b_half[side] = pack(compose(*nodes))

    swap = remote(b_half.at[side], b_half.at[side], s_half, r_half, at_core())
    swap.start()
    leaf = remote(b_z.at[sibling], b_z.at[sibling], s_sib.at[0], r_sib.at[0], at_core())
    near = remote(z_near, z_near, s_sib.at[1], r_sib.at[1], at_core())

    @pl.when(home == side)
    def _():
        z_near[...] = z_pairs[1 - (zz % half) // 2]
        leaf.start()
        near.start()

    swap.wait()

    @fence
    def _():
        b_x[x] = pack(compose(unpack(b_half[0]), unpack(b_half[1])))

    xs = ring(b_x, x, at_x, s_x, r_x)

    @pl.when(home == side)
    def _():
        leaf.wait_send()
        near.wait_send()

    @pl.when(home != side)
    def _():
        leaf.wait_recv()
        near.wait_recv()

    @fence
    def _():
        before, after = sides[0], sides[1]
        before, after = narrow(zz % 2 == 1, unpack(b_z[sibling]), before, after)
        before, after = narrow((zz % half) // 2 == 1, z_near[...], before, after)
        before, after = narrow(home == 1, unpack(b_half[1 - home]), before, after)
        sides[0] = before
        sides[1] = after

    finish(xs)

    t = b_x[0, 0:R]
    p = jnp.zeros((R, U), F32)
    ends = [t]
    for j in range(1, nx):
        p = jnp.where(x == j, t[:, :U], p)
        t = dot3(t[:, :U], b_x[j, R:N1]) + b_x[j, 0:R]
        ends.append(t)
    q_run = ends[nx - 1][:, U:]
    q = jnp.zeros((R, U), F32)
    for j in reversed(range(nx - 1)):
        q = jnp.where(x == j, q_run, q)
        if j:
            q_run = dot3(q_run, unpack(b_x[j])[N1:, U:]) + ends[j][:, U:]
    own = unpack(b_core[side])
    before, after = sides[0], sides[1]
    p = dot3(p, before[R:N1, :U]) + before[:R, :U]
    t = dot3(p, own[R:N1, :U]) + own[:R, :U]
    t = dot3(t, after[R:N1]) + after[:R]
    q = t[:, U:] + dot3(q, after[N1:, U:])
    out[...] = zbuf[0:R, :] + dot3(jnp.concatenate([p, q], axis=1), zbuf[R:, :])


def local(levels, interpret, rhs, lower, lcols, upper, ucols, diag, llow, lup, counts):
    vmem = pl.BlockSpec(memory_space=pltpu.VMEM)
    anywhere = pl.BlockSpec(memory_space=pl.ANY)
    dma = pltpu.SemaphoreType.DMA
    lower = jnp.transpose(lower, (1, 0, 2))
    upper = jnp.transpose(upper, (1, 0, 2))
    diag, llow, lup = diag[None], llow[None], lup[None]
    cols = NB * U
    lcols, ucols, rhs = (pltpu.with_memory_space_constraint(v, pltpu.HBM) for v in (lcols, ucols, rhs))
    lower, upper, diag, llow, lup = (pltpu.with_memory_space_constraint(v, pltpu.HBM) for v in (lower, upper, diag, llow, lup))
    scratch = [
        pltpu.VMEM((2, 32, 8, U * U), BF16),
        pltpu.VMEM((72 * PITCH, 128), F32),
        pltpu.VMEM((72 * PITCH, 128), F32),
        pltpu.VMEM((N2, cols), F32),
        pltpu.VMEM((N2, cols), F32),
        pltpu.VMEM((U, cols), F32),
        pltpu.VMEM((U, cols), F32),
        pltpu.VMEM((4, 256, 256), F32),
        pltpu.VMEM((4, 256, 256), F32),
        dma((5, 2 * CHUNKS)),
        pltpu.VMEM((R, cols), F32),
        pltpu.VMEM((NB, KL), jnp.int32),
        pltpu.VMEM((NB, KL), jnp.int32),
        dma((3,)),
        pltpu.VMEM((2, 144, 256), BF16),
        pltpu.VMEM((2, PIECE, 144, 256), F32),
    ]
    if levels is None:
        outs = (jax.ShapeDtypeStruct((PACKED, 128), F32), jax.ShapeDtypeStruct((N2, cols), F32))
        params = pltpu.CompilerParams(vmem_limit_bytes=48000000)
    else:
        nx, nz, ny = levels
        outs = jax.ShapeDtypeStruct((R, cols), F32)
        scratch += [pltpu.VMEM((n, PACKED, 128), F32) for n in (2, ny, nz, nx, 2)]
        scratch += [pltpu.VMEM(m + (N2, 128), F32) for m in ((ny // 2,), (nz // 4,), (), (2,))]
        scratch += [dma] * 4 + [dma((2,))] * 2 + [dma((n - 1,)) for n in (ny, ny, nz, nz, nx, nx)]
        params = pltpu.CompilerParams(
            collective_id=0, has_side_effects=True, vmem_limit_bytes=48000000
        )
    return pl.pallas_call(
        functools.partial(kernel, levels),
        out_shape=outs,
        in_specs=[anywhere] * 8 + [pl.BlockSpec(memory_space=pltpu.SMEM)],
        out_specs=jax.tree.map(lambda _: vmem, outs),
        scratch_shapes=scratch,
        compiler_params=params,
        interpret=interpret,
        name="ilu_apply",
    )(rhs, lower, upper, diag, llow, lup, lcols, ucols, counts)


def solution(mesh, levels=LEVELS):
    both = ("chain", "side")
    return jax.shard_map(
        functools.partial(local, levels, False),
        mesh=mesh,
        in_specs=(
            P(None, both),
            P(both, None, None),
            P(both, None),
            P(both, None, None),
            P(both, None),
            P(both, None),
            P(both, None),
            P(both, None),
            P(both),
        ),
        out_specs=P(None, both),
        check_vma=False,
    )
```
